32 devices in a mesh: prow: 8 (over z, x), pcol: 4 (over y, core).
Axes of the slice: x: 2, y: 2, z: 4, core: 2. Of those that a mesh axis runs over, the one named last changes fastest.
Arguments:
- inverse_pool: float32 [1536, 1536], P('prow', 'pcol'), may hold values from -6 to 6
- panel_one: float32 [1536, 512], P(('prow', 'pcol')), may hold values from -0.1875 to 0.1875
- panel_two: float32 [1536, 512], P(('prow', 'pcol')), may hold values from -0.21875 to 0.21875
- upper_two: float32 [512, 512], replicated, may hold values from -0.25 to 0.25
- lower_one: float32 [512, 512], replicated, as said below
- lower_two: float32 [512, 512], replicated, as said below
- list_one: int32 [9], replicated, may hold values from 0 to 11, as said below
- list_two: int32 [6], replicated, may hold values from 0 to 11, as said below
Outputs:
- first_offdiag: float32 [1536, 512], P(('prow', 'pcol'))
- first_diag: float32 [512, 512], replicated
- second_offdiag: float32 [1536, 512], P(('prow', 'pcol'))
- second_coupling: float32 [512, 512], replicated
- second_diag: float32 [512, 512], replicated
The draws below stay inside these ranges and needn't reach their ends.
Inputs may be any that keep to these rules, and one draw needn't show every extreme that they name: `list_one`: distinct block numbers, among them 0, 6 and 11. `list_two`: distinct block numbers, each of which is also in list_one, among them 0, 6 and 11. `lower_one`: lower triangular with a diagonal of 1 to 1.5. `lower_two`: lower triangular with a diagonal of 1 to 1.5.
All inputs are finite; a program needn't handle non-finite values.
Results may differ from the reference program's by a relative error of at most 0.000073.
Values sent between devices are 32-bit elements; how exact they have to be, the bound alone decides.
A program may use at most 64 MiB of HBM per device.

```python
import jax
import jax.numpy as jnp
from jax import lax

W = 512
BLK = 128
NP = 1536
NBLK = 12
NSEL1 = 9
NSEL2 = 6


def lower_factor(key):
    strict = jax.random.normal(jax.random.fold_in(key, 3), (W, W), jnp.float32) * (0.6 / W ** 0.5)
    diagonal = 1.0 + 0.5 * jax.random.uniform(jax.random.fold_in(key, 4), (W,), jnp.float32)
    return jnp.tril(strict, -1) + jnp.diag(diagonal)


def draw_lower_one(key, part):
    return lower_factor(jax.random.fold_in(key, 21))


def draw_lower_two(key, part):
    return lower_factor(jax.random.fold_in(key, 22))


def ancestor_order(key):
    shuffled = jax.random.permutation(jax.random.fold_in(key, 11), NBLK).astype(jnp.int32)
    blocks = jnp.arange(NBLK, dtype=jnp.int32)
    middle = NP // 2 // BLK
    scores = shuffled + 3
    scores = jnp.where(blocks == 0, 0, scores)
    scores = jnp.where(blocks == middle, 1, scores)
    scores = jnp.where(blocks == NBLK - 1, 2, scores)
    return jnp.argsort(scores, stable=True).astype(jnp.int32)


def draw_list_one(key, part):
    chosen = ancestor_order(key)[:NSEL1]
    return jax.random.permutation(jax.random.fold_in(key, 13), chosen).astype(jnp.int32)


def draw_list_two(key, part):
    chosen = ancestor_order(key)[:NSEL2]
    return jax.random.permutation(jax.random.fold_in(key, 12), chosen).astype(jnp.int32)


def block_levels(rng, shape, split, low, top_value):
    def one(dim, parts):
        draws = jax.random.uniform(jax.random.fold_in(jax.random.fold_in(rng, 6), dim), (parts,), jnp.float32, low / len(split), top_value / len(split))
        return jnp.repeat(jnp.exp(draws), shape[dim] // parts).reshape((-1,) + (1,) * (len(shape) - dim - 1))

    factor_of = one(*split[0])
    for cut in split[1:]:
        factor_of = factor_of * one(*cut)
    return factor_of


def centred(own_key, extent, deviation, reach, shards=(), kind=jnp.bfloat16):
    loudness = block_levels(own_key, extent, shards, -0.22, 0.18) if shards else 1.0
    drawn = jax.random.normal(own_key, extent, jnp.float32) * deviation * loudness
    return jnp.minimum(jnp.maximum(drawn, -reach), reach).astype(kind)


def setup_inputs(seed: int = 0) -> dict:
    streams_of = jax.random.split(jax.random.key(seed), 9)
    inverse_pool = centred(streams_of[0], (NP, NP), 1.0, 6.0, ((0, 8), (1, 4)), jnp.float32)
    panel_one = centred(streams_of[1], (NP, W), (NSEL1 * BLK) ** -0.5, 0.1875, ((0, 32),), jnp.float32)
    panel_two = centred(streams_of[2], (NP, W), (NSEL2 * BLK) ** -0.5, 0.21875, ((0, 32),), jnp.float32)
    upper_two = centred(streams_of[3], (W, W), W ** -0.5, 0.25, (), jnp.float32)
    lower_one = draw_lower_one(jax.random.fold_in(streams_of[8], 71), 0)
    lower_two = draw_lower_two(jax.random.fold_in(streams_of[8], 71), 0)
    list_one = draw_list_one(jax.random.fold_in(streams_of[8], 71), 0)
    list_two = draw_list_two(jax.random.fold_in(streams_of[8], 71), 0)
    return dict(inverse_pool=inverse_pool, panel_one=panel_one, panel_two=panel_two, upper_two=upper_two, lower_one=lower_one, lower_two=lower_two, list_one=list_one, list_two=list_two)


def product(left, right):
    return jnp.dot(left, right, precision=lax.Precision.HIGHEST, preferred_element_type=jnp.float32)


def transposed_product(left, right):
    return lax.dot_general(left, right, (((0,), (0,)), ((), ())), precision=lax.Precision.HIGHEST, preferred_element_type=jnp.float32)


def live_rows(listing):
    blocks = jnp.arange(NP, dtype=jnp.int32) // BLK
    hits = jnp.any(blocks[:, None] == listing[None, :].astype(jnp.int32), axis=1)
    return jnp.where(hits, 1.0, 0.0).astype(jnp.float32)[:, None]


def reference(inverse_pool, panel_one, panel_two, upper_two, lower_one, lower_two, list_one, list_two):
    live_one = live_rows(list_one)
    live_two = live_rows(list_two)
    masked_one = live_one * panel_one
    masked_two = live_two * panel_two
    first_offdiag = -live_one * product(inverse_pool, masked_one)
    first_diag = transposed_product(lower_one, lower_one) - transposed_product(masked_one, first_offdiag)
    second_offdiag = -live_two * (product(first_offdiag, upper_two) + product(inverse_pool, masked_two))
    second_coupling = -(product(first_diag, upper_two) + transposed_product(first_offdiag, masked_two))
    second_diag = transposed_product(lower_two, lower_two) - transposed_product(upper_two, second_coupling) - transposed_product(masked_two, second_offdiag)
    return first_offdiag, first_diag, second_offdiag, second_coupling, second_diag
```

```python
import functools

import jax
import jax.numpy as jnp
from jax import lax
from jax.experimental import pallas as pl
from jax.experimental.pallas import tpu as pltpu
from jax.sharding import PartitionSpec as P

BLK = 128
MESH = pl.DeviceIdType.MESH


def halves(value):
    high = value.astype(jnp.bfloat16)
    low = (value - high.astype(jnp.float32)).astype(jnp.bfloat16)
    return high, low


def split_dot(left, right, dims):
    def one(a, b):
        return lax.dot_general(a, b, (dims, ((), ())), preferred_element_type=jnp.float32)

    return one(left[0], right[0]) + (one(left[0], right[1]) + one(left[1], right[0]))


PLAIN = ((1,), (0,))
FIRST = ((0,), (0,))


def live_column(listing, first_row, count):
    blocks = (first_row + lax.broadcasted_iota(jnp.int32, (count, 1), 0)) // BLK

    def step(k, hits):
        return jnp.maximum(hits, jnp.where(blocks == listing[k], 1.0, 0.0).astype(jnp.float32))

    return lax.fori_loop(0, listing.shape[0], step, jnp.zeros((count, 1), jnp.float32))


def write_out(*refs):
    sems = refs[-1]
    copies = [pltpu.make_async_copy(refs[k], refs[5 + k], sems.at[k]) for k in range(5)]
    for copy in copies:
        copy.start()
    for copy in copies:
        copy.wait()


def body(
    R, C, nsend,
    x_in, one_in, two_in, u_in, l1_in, l2_in, list1, list2,
    f_out, d1_out, s_out, c_out, d2_out,
    x_v, u_v, l1_v, l2_v, zbuf, mcol, mrow, abuf, arecv, brecv, asum, frow, qbuf, xrecv, xsum, zrecv, qfull, wt,
    load_sem, send_sem, z_sem, m_sem, g_sem, a_sem, b_sem, f_sem, x_sem, q_sem, gz_sem, gx_sem, gy_sem, gc_sem,
):
    g, half = R // C, C // 2
    span, W = one_in.shape
    rows, K = x_in.shape
    wc = W // C
    part, ch = W // g, W // R
    p, c = lax.axis_index("prow"), lax.axis_index("pcol")
    z, i = p // g, p % g
    partner = c + 1 - 2 * (c % 2)
    panels = (one_in, two_in)
    pending = []

    def send(src, dst, recv_sem, to, when=None):
        copy = pltpu.make_async_remote_copy(
            src_ref=src, dst_ref=dst, send_sem=send_sem.at[len(pending)],
            recv_sem=recv_sem, device_id=to, device_id_type=MESH,
        )
        pending.append((copy, when))
        if when is None:
            copy.start()
        else:
            pl.when(when)(copy.start)

    def arrived(dst, recv_sem):
        pltpu.make_async_copy(dst, dst, recv_sem).wait()

    def at(base, index, size):
        return base.at[pl.ds(pl.multiple_of(index * size, 8), size)]

    def plane_peer(dz):
        return (((z + dz) % C) * g + i, c)

    def side_peer(di):
        return (z * g + (i + di) % g, c)

    loads = []
    for k, (src, dst) in enumerate(((l1_in, l1_v), (l2_in, l2_v), (x_in, x_v), (u_in, u_v))):
        copy = pltpu.make_async_copy(src, dst, load_sem.at[k])
        copy.start()
        loads.append(copy)

    barrier = pltpu.get_barrier_semaphore()
    peers = 0
    for dp in range(1, R):
        pl.semaphore_signal(barrier, inc=1, device_id=((p + dp) % R, c), device_id_type=MESH)
        peers += 1
    for di in range(g):
        for dc in range(1, C):
            pl.semaphore_signal(
                barrier, inc=1, device_id=(z * g + (i + di) % g, (c + dc) % C), device_id_type=MESH
            )
            peers += 1
    pl.semaphore_wait(barrier, peers)

    def to_columns(k, src, plane, valid=True):
        own = i * C + c
        dst, sem = at(mcol.at[k], own, span), m_sem.at[k, own]
        send(src, dst, sem, (p, plane), (plane != c) & valid)
        pl.when((plane == c) & valid)(pltpu.make_async_copy(src, dst, sem).start)
        for di in range(1, g):
            to = (z * g + (i + di) % g, plane)
            send(src, dst, sem, to, (plane // 2 == c // 2) & valid)

    def along(k, src, plane, way, valid=True):
        inside = (z + 1 < C) if way > 0 else (z > 0)
        send(src, zbuf.at[k, plane], z_sem.at[k, plane], plane_peer(way % C), inside & valid)

    def far(dy, parity):
        return ((c // 2 + dy) % half) * 2 + parity

    def across(k):
        for dy in range(1, half):
            for parity in range(2):
                slot = i * C + far(dy, parity)
                piece = at(mcol.at[k], slot, span)
                arrived(piece, m_sem.at[k, slot])
                for di in range(1, g):
                    send(piece, piece, m_sem.at[k, slot], side_peer(di))

    def columns_arrived(k):
        for dy in range(half):
            for parity in range(2):
                for di in range(1 if dy else 0, g):
                    slot = ((i + di) % g) * C + far(dy, parity)
                    arrived(at(mcol.at[k], slot, span), m_sem.at[k, slot])

    def to_row(k):
        dst, sem = at(mrow.at[k], c, span), g_sem.at[k, c]
        pltpu.make_async_copy(panels[k], dst, sem).start()
        for dc in range(2, C, 2):
            send(panels[k], dst, sem, (p, (c + dc) % C))
        send(panels[k], dst, sem, (p, partner))

    def row_onward(k):
        for dc in range(2, C, 2):
            other = (c + dc) % C
            piece = at(mrow.at[k], other, span)
            arrived(piece, g_sem.at[k, other])
            send(piece, piece, g_sem.at[k, other], (p, partner))

    def row_arrived(k):
        arrived(at(mrow.at[k], c, span), g_sem.at[k, c])
        for dc in range(0, C, 2):
            other = (partner + dc) % C
            arrived(at(mrow.at[k], other, span), g_sem.at[k, other])

    def tile_product(k, listing):
        columns_arrived(k)
        masked = live_column(listing, c * K, K) * mcol[k]
        product = split_dot(x_pair, halves(masked), PLAIN)
        for cc in range(C):
            abuf[k, cc] = product[:, cc * wc:(cc + 1) * wc]
        for j in range(half):
            send(abuf.at[k, (partner + 2 * j) % C], arecv.at[k, j], a_sem.at[k, j], (p, partner))

    def pair_sum(k):
        for j in list(range(1, half)) + [0]:
            other = (c + 2 * j) % C
            arrived(arecv.at[k, j], a_sem.at[k, j])
            abuf[k, other] = abuf[k, other] + arecv[k, j]
            if j:
                send(abuf.at[k, other], brecv.at[k, j], b_sem.at[k, j], (p, other))

    def total(k, mask):
        result = abuf[k, c]
        for j in range(1, half):
            arrived(brecv.at[k, j], b_sem.at[k, j])
            result = result + brecv[k, j]
        result = mask * result
        asum[k] = result
        return halves(result)

    def rows_out(k):
        for dc in range(1, C):
            other = (c + dc) % C
            send(at(asum.at[k], other, span), frow.at[k, c], f_sem.at[k, c], (p, other))
        frow[k, c] = asum[k, pl.ds(pl.multiple_of(c * span, 8), span)]

    def side_out(b):
        for di in range(1, g):
            other = (i + di) % g
            send(at(qbuf.at[b], other, part), xrecv.at[b, di], x_sem.at[b, di], side_peer(di))

    def side_in(b):
        result = qbuf[b, pl.ds(pl.multiple_of(i * part, 8), part)]
        for di in range(1, g):
            arrived(xrecv.at[b, di], x_sem.at[b, di])
            result = result + xrecv[b, di]
        xsum[b] = result
        for dz in range(1, C):
            send(at(xsum.at[b], (z + dz) % C, ch), zrecv.at[b, dz], q_sem.at[b, dz], plane_peer(dz))

    def block(b, column, side, plane):
        first = b * W + side * part + plane * ch
        return qfull.at[column, pl.ds(pl.multiple_of(first, 8), ch)]

    def block_part(b, column, side):
        return qfull.at[column, pl.ds(pl.multiple_of(b * W + side * part, 8), part)]

    def plane_in(b):
        result = xsum[b, pl.ds(pl.multiple_of(z * ch, 8), ch)]
        for dz in range(1, C):
            arrived(zrecv.at[b, dz], q_sem.at[b, dz])
            result = result + zrecv[b, dz]
        piece = block(b, c, i, z)
        piece[...] = result
        for dz in range(1, C):
            send(piece, piece, gz_sem.at[b, dz], plane_peer(dz))

    def gram_part(b, di, dc, base):
        return block_part(b, (base + C - dc) % C, (i + g - di) % g)

    def to_side(b, dc):
        piece = gram_part(b, 0, dc, c)
        for di in range(1, g):
            send(piece, piece, gx_sem.at[b, di, dc // 2], side_peer(di))

    def to_rows(b, di):
        piece = gram_part(b, di, 0, c)
        for dc in range(2, C, 2):
            send(piece, piece, gy_sem.at[b, di, dc // 2], (p, (c + dc) % C))

    def to_partner(b, di, dc):
        piece = gram_part(b, di, dc, c)
        send(piece, piece, gc_sem.at[b, di, dc // 2], (p, partner))

    def side_arrived(b, di, dc):
        arrived(gram_part(b, di, dc, c), gx_sem.at[b, di, dc // 2])

    def rows_arrived(b, di, dc):
        arrived(gram_part(b, di, dc, c), gy_sem.at[b, di, dc // 2])

    def gather_side(b):
        for dz in range(1, C):
            arrived(block(b, c, i, (z + C - dz) % C), gz_sem.at[b, dz])
        to_side(b, 0)
        to_rows(b, 0)
        to_partner(b, 0, 0)

    def gather_row(b):
        if b == 1:
            for dc in range(2, C, 2):
                rows_arrived(b, 0, dc)
                to_side(b, dc)
                to_partner(b, 0, dc)
        else:
            for di in range(1, g):
                side_arrived(b, di, 0)
                to_rows(b, di)
                to_partner(b, di, 0)

    def gather_core(b):
        if b == 1:
            for di in range(1, g):
                for dc in range(0, C, 2):
                    side_arrived(b, di, dc)
                    to_partner(b, di, dc)
        else:
            for di in range(g):
                for dc in range(2, C, 2):
                    rows_arrived(b, di, dc)
                    to_partner(b, di, dc)

    def gathered(b):
        for di in range(g):
            for dc in range(0, C, 2):
                piece = block_part(b, (partner + C - dc) % C, (i + g - di) % g)
                arrived(piece, gc_sem.at[b, di, dc // 2])

    for k in range(2):
        along(k, panels[k], z, 1)
        along(k, panels[k], z, -1)
        to_columns(k, panels[k], z)
    for k in range(2):
        for dz in range(1, C):
            for way in (1, -1):
                valid = (z >= dz) if way > 0 else (z + dz < C)
                plane = (z + C - way * dz) % C
                src, sem = zbuf.at[k, plane], z_sem.at[k, plane]
                pl.when(valid)(functools.partial(arrived, src, sem))
                if dz < C - 1:
                    along(k, src, plane, way, valid)
                to_columns(k, src, plane, valid)
        to_row(k)
        if k == 0:
            across(0)
            for copy in loads[2:]:
                copy.wait()
            x_pair = halves(x_v[...])
            row_one, row_two = live_column(list1, p * rows, rows), live_column(list2, p * rows, rows)
    row_onward(0)
    tile_product(0, list1)
    across(1)
    pair_sum(0)
    row_onward(1)
    row_arrived(0)
    left = halves(row_one * mrow[0])
    right_one = total(0, row_one)
    qbuf[0] = split_dot(left, right_one, FIRST)
    side_out(0)
    for copy in loads[:2]:
        copy.wait()
    for src, dst in ((l1_v, d1_out), (l2_v, d2_out)):
        pair = halves(src[...])
        dst[...] = split_dot(pair, pair, FIRST)
    tile_product(1, list2)
    pair_sum(1)
    row_arrived(1)
    left = halves(row_two * mrow[1])
    cross = split_dot(right_one, left, FIRST)
    for cc in range(C):
        qbuf[1, cc * wc:(cc + 1) * wc] = cross[:, cc * wc:(cc + 1) * wc]
    side_out(1)
    side_in(0)
    right_two = total(1, row_two)
    qbuf[2] = split_dot(left, right_two, FIRST)
    side_out(2)
    plane_in(0)
    side_in(1)
    gather_side(0)
    plane_in(1)
    side_in(2)
    gather_row(0)
    gather_side(1)
    plane_in(2)
    gather_core(0)
    gather_row(1)
    gather_side(2)
    rows_out(0)
    rows_out(1)
    gather_core(1)
    gather_row(2)

    u_pair = halves(u_v[...])
    gathered(0)
    for cc in range(C):
        d1_out[:, cc * wc:(cc + 1) * wc] += qfull[cc, 0:W]
    d1_u = split_dot(halves(d1_out[...]), u_pair, PLAIN)
    gather_core(2)
    for k in range(2):
        for dc in range(1, C):
            other = (c + dc) % C
            arrived(frow.at[k, other], f_sem.at[k, other])
    for cc in range(C):
        f_out[:, cc * wc:(cc + 1) * wc] = -frow[0, cc]
        s_out[:, cc * wc:(cc + 1) * wc] = frow[1, cc]
    f_u = split_dot(halves(f_out[...]), u_pair, PLAIN)
    s_out[...] = -live_column(list2, p * rows + c * span, span) * (f_u + s_out[...])

    gathered(1)
    for cc in range(C):
        for k in range(C):
            wt[cc * wc:(cc + 1) * wc, k * wc:(k + 1) * wc] = qfull[cc, W + k * wc:W + (k + 1) * wc]
    c_out[...] = wt[...] - d1_u
    d2_out[...] -= split_dot(u_pair, halves(c_out[...]), FIRST) + split_dot(
        halves(wt[...]), u_pair, FIRST
    )
    gathered(2)
    for cc in range(C):
        d2_out[:, cc * wc:(cc + 1) * wc] += qfull[cc, 2 * W:3 * W]

    assert len(pending) <= nsend
    for copy, when in pending:
        if when is None:
            copy.wait_send()
        else:
            pl.when(when)(copy.wait_send)


def fast_body(
    R, C, nsend,
    x_in, one_in, two_in, u_in, l1_in, l2_in, list1, list2,
    f_out, d1_out, s_out, c_out, d2_out,
    x_v, u_v, l1_v, l2_v, mcol, mrow, abuf, arecv, asum, frow, qbuf, krecv, ksum, zrecv, qfull, wt,
    load_sem, send_sem, x_sem, m_sem, g_sem, a_sem, f_sem, k_sem, q_sem, gz_sem, gx_sem, gy_sem, gd_sem, gc_sem,
):
    span, W = one_in.shape
    rows, K = x_in.shape
    wc = W // C
    Z = R // 2
    part, ch = W // 2, W // R
    p, c = lax.axis_index("prow"), lax.axis_index("pcol")
    z, x, y, k = p // 2, p % 2, c // 2, c % 2
    slab = 2 * y + x
    panels = (one_in, two_in)
    others = ((1, 0), (0, 1), (1, 1))
    pending = []

    def dev(x, y, z, k):
        return (z * 2 + x, y * 2 + k)

    def send(src, dst, recv_sem, to, when=None):
        copy = pltpu.make_async_remote_copy(
            src_ref=src, dst_ref=dst, send_sem=send_sem.at[len(pending)],
            recv_sem=recv_sem, device_id=to, device_id_type=MESH,
        )
        pending.append((copy, when))
        if when is None:
            copy.start()
        else:
            pl.when(when)(copy.start)

    def arrived(dst, recv_sem):
        pltpu.make_async_copy(dst, dst, recv_sem).wait()

    def at(base, index, size):
        return base.at[pl.ds(pl.multiple_of(index * size, 8), size)]

    def send_or_copy(src, dst, sem, to, here):
        send(src, dst, sem, to, jnp.logical_not(here))
        pl.when(here)(pltpu.make_async_copy(src, dst, sem).start)

    pl.when(k == x)(pltpu.make_async_copy(x_in, x_v, x_sem).start)
    loads = []
    for n, (src, dst) in enumerate(((l1_in, l1_v), (l2_in, l2_v), (u_in, u_v))):
        copy = pltpu.make_async_copy(src, dst, load_sem.at[n])
        copy.start()
        loads.append(copy)

    barrier = pltpu.get_barrier_semaphore()

    def greet(to):
        pl.semaphore_signal(barrier, inc=1, device_id=to, device_id_type=MESH)

    @pl.when(slab != z)
    def _():
        for sx in range(2):
            for sy in range(2):
                greet(dev(sx, sy, slab, k))

    for dz in range(1, Z):
        greet(dev(x, y, (z + dz) % Z, k))
    for d in range(1, 8):
        greet(dev((x + d % 2) % 2, (y + d // 2 % 2) % 2, z, (k + d // 4) % 2))
    pl.semaphore_wait(barrier, 7 + 2 * (Z - 1))

    own = x * C + c

    def in_columns(b, slot):
        return at(mcol.at[b], slot, span), m_sem.at[b, slot]

    def panel_out(b):
        px, py = z % 2, z // 2
        dst, sem = in_columns(b, own)
        for dz in (2, 3, 1):
            send(panels[b], dst, sem, dev(px, py, (z + dz) % Z, k))
        send_or_copy(panels[b], dst, sem, dev(px, py, z, k), (x == px) & (y == py))

    def left_out(b):
        dst, sem = at(mrow.at[b], c, span), g_sem.at[b, c]
        for dx, dy in others:
            send(panels[b], dst, sem, dev((x + dx) % 2, (y + dy) % 2, z, x))
        send_or_copy(panels[b], dst, sem, dev(x, y, z, 1 - k), k == x)

    def columns_in(b):
        for sx in range(2):
            for sy in range(2):
                piece, sem = in_columns(b, sx * C + 2 * sy + k)
                arrived(piece, sem)
                send(piece, piece, sem, dev(x, y, z, 1 - k))

    def columns_arrived(b):
        for sx in range(2):
            for sy in range(2):
                arrived(*in_columns(b, sx * C + 2 * sy + 1 - k))

    def left_arrived(b):
        for n in range(C):
            arrived(at(mrow.at[b], n, span), g_sem.at[b, n])

    def tile_product(b, listing):
        masked = live_column(listing, slab * K, K) * mcol[b]
        product = split_dot(x_pair, halves(masked), PLAIN)
        for n in range(C):
            abuf[b, n] = product[:, n * wc:(n + 1) * wc]
        for n, (dx, dy) in enumerate(others):
            tx, ty = (x + dx) % 2, (y + dy) % 2
            send(abuf.at[b, 2 * ty + tx], arecv.at[b, n], a_sem.at[b, n], dev(tx, ty, z, k))

    def total(b, mask):
        result = abuf[b, slab]
        for n in range(len(others)):
            arrived(arecv.at[b, n], a_sem.at[b, n])
            result = result + arecv[b, n]
        result = mask * result
        asum[b] = result
        return halves(result)

    def rows_out(b):
        for dy in range(2):
            for dk in range(2):
                ty, tk = (y + dy) % 2, (k + dk) % 2
                src, dst, sem = at(asum.at[b], 2 * ty + tk, span), frow.at[b, slab], f_sem.at[b, slab]
                if dy or dk:
                    send(src, dst, sem, dev(k, ty, z, tk))
                else:
                    send_or_copy(src, dst, sem, dev(k, ty, z, tk), k == x)

    def core_out(b):
        send(at(qbuf.at[b], 1 - k, part), krecv.at[b], k_sem.at[b], dev(x, y, z, 1 - k))

    def core_in(b):
        arrived(krecv.at[b], k_sem.at[b])
        ksum[b] = qbuf[b, pl.ds(pl.multiple_of(k * part, 8), part)] + krecv[b]
        for dz in range(1, Z):
            to = (z + dz) % Z
            send(at(ksum.at[b], to, ch), zrecv.at[b, dz], q_sem.at[b, dz], dev(x, y, to, k))

    def region(b, column, core):
        return qfull.at[column, pl.ds(pl.multiple_of(b * W + core * part, 8), part)]

    def chunk(b, column, core, dz):
        plane = (z + Z - dz) % Z
        return qfull.at[column, pl.ds(pl.multiple_of(b * W + core * part + plane * ch, 8), ch)]

    beside, along, across = 2 * y + 1 - x, 2 * (1 - y) + x, 2 * (1 - y) + 1 - x

    def to_core(piece, sem):
        send(piece, piece, sem, dev(x, y, z, 1 - k))

    def to_near(b, dz):
        piece = chunk(b, slab, k, dz)
        send(piece, piece, gx_sem.at[b, dz], dev(1 - x, y, z, k))
        send(piece, piece, gy_sem.at[b, dz], dev(x, 1 - y, z, k))

    def planes_in(b):
        result = ksum[b, pl.ds(pl.multiple_of(z * ch, 8), ch)]
        for dz in range(1, Z):
            arrived(zrecv.at[b, dz], q_sem.at[b, dz])
            result = result + zrecv[b, dz]
        piece = chunk(b, slab, k, 0)
        piece[...] = result
        for dz in range(1, Z):
            send(piece, piece, gz_sem.at[b, dz], dev(x, y, (z + dz) % Z, k))
        to_near(b, 0)

    def planes_on(b):
        for dz in range(1, Z):
            arrived(chunk(b, slab, k, dz), gz_sem.at[b, dz])
            to_near(b, dz)
        to_core(region(b, slab, k), gc_sem.at[b, 0])

    def near_on(b, dz):
        piece = chunk(b, beside, k, dz)
        arrived(piece, gx_sem.at[b, dz])
        if dz % 2 == 0:
            send(piece, piece, gd_sem.at[b, dz], dev(x, 1 - y, z, k))
        piece = chunk(b, along, k, dz)
        arrived(piece, gy_sem.at[b, dz])
        if dz % 2 == 1:
            send(piece, piece, gd_sem.at[b, dz], dev(1 - x, y, z, k))

    def near_rest(b):
        for dz in range(1, Z):
            near_on(b, dz)
        to_core(region(b, beside, k), gc_sem.at[b, 1])
        to_core(region(b, along, k), gc_sem.at[b, 2])

    def gather_far(b):
        for dz in range(Z):
            arrived(chunk(b, across, k, dz), gd_sem.at[b, dz])
        to_core(region(b, across, k), gc_sem.at[b, 3])

    def gathered(b):
        for n, column in enumerate((slab, beside, along, across)):
            arrived(region(b, column, 1 - k), gc_sem.at[b, n])

    def square(n, src, dst):
        loads[n].wait()
        pair = halves(src[...])
        dst[...] = split_dot(pair, pair, FIRST)

    panel_out(0)
    send(x_in, x_v, x_sem, dev(1 - x, y, z, 1 - k), k != x)
    panel_out(1)
    square(0, l1_v, d1_out)
    left_out(0)
    square(1, l2_v, d2_out)
    block_row = 2 * z + k
    row_one, row_two = live_column(list1, block_row * rows, rows), live_column(list2, block_row * rows, rows)
    arrived(x_v, x_sem)
    x_pair = halves(x_v[...])
    columns_in(0)
    columns_arrived(0)
    tile_product(0, list1)
    columns_in(1)
    columns_arrived(1)
    left_out(1)
    tile_product(1, list2)
    left_arrived(0)
    left_one = halves(row_one * mrow[0])
    right_one = total(0, row_one)
    qbuf[0] = split_dot(left_one, right_one, FIRST)
    core_out(0)
    left_arrived(1)
    left_two = halves(row_two * mrow[1])
    cross = split_dot(right_one, left_two, FIRST)
    for n in range(C):
        qbuf[1, n * wc:(n + 1) * wc] = cross[:, n * wc:(n + 1) * wc]
    core_out(1)
    core_in(0)
    core_in(1)
    right_two = total(1, row_two)
    qbuf[2] = split_dot(left_two, right_two, FIRST)
    core_out(2)
    planes_in(0)
    core_in(2)
    planes_in(1)
    planes_on(0)
    planes_in(2)
    near_on(0, 0)
    planes_on(1)
    near_on(1, 0)
    near_rest(0)
    planes_on(2)
    near_on(2, 0)
    near_rest(1)
    gather_far(0)
    rows_out(0)
    rows_out(1)
    near_rest(2)
    gather_far(1)

    loads[2].wait()
    u_pair = halves(u_v[...])
    gathered(0)
    for n in range(C):
        d1_out[:, n * wc:(n + 1) * wc] += qfull[n, 0:W]
    gather_far(2)
    d1_u = split_dot(halves(d1_out[...]), u_pair, PLAIN)
    for b in range(2):
        for n in range(C):
            arrived(frow.at[b, n], f_sem.at[b, n])
    for n in range(C):
        f_out[:, n * wc:(n + 1) * wc] = -frow[0, n]
        s_out[:, n * wc:(n + 1) * wc] = frow[1, n]
    f_u = split_dot(halves(f_out[...]), u_pair, PLAIN)
    s_out[...] = -live_column(list2, p * rows + c * span, span) * (f_u + s_out[...])

    gathered(1)
    for n in range(C):
        for m in range(C):
            wt[n * wc:(n + 1) * wc, m * wc:(m + 1) * wc] = qfull[n, W + m * wc:W + (m + 1) * wc]
    c_out[...] = wt[...] - d1_u
    d2_out[...] -= split_dot(u_pair, halves(c_out[...]), FIRST) + split_dot(
        halves(wt[...]), u_pair, FIRST
    )
    gathered(2)
    for n in range(C):
        d2_out[:, n * wc:(n + 1) * wc] += qfull[n, 2 * W:3 * W]

    assert len(pending) <= nsend
    for copy, when in pending:
        if when is None:
            copy.wait_send()
        else:
            pl.when(when)(copy.wait_send)


def solution(mesh):
    R, C = mesh.shape["prow"], mesh.shape["pcol"]
    g = R // C
    f32, dma = jnp.float32, pltpu.SemaphoreType.DMA

    def general(span, rows, K, W):
        wc, half = W // C, C // 2
        panel = 2 * (C - 1) + (2 * C - 1) * g + 2 * (half - 1) * (g - 1) + half + (half - 1)
        reduced = half + (half - 1) + (C - 1)
        gram = (g - 1) + 2 * (C - 1) + (g - 1) + g * half + g * (half - 1)
        nsend = 2 * panel + 2 * reduced + 3 * gram
        return functools.partial(body, R, C, nsend), [
            pltpu.VMEM((rows, K), f32),
            pltpu.VMEM((W, W), f32),
            pltpu.VMEM((W, W), f32),
            pltpu.VMEM((W, W), f32),
            pltpu.VMEM((2, C, span, W), f32),
            pltpu.VMEM((2, K, W), f32),
            pltpu.VMEM((2, rows, W), f32),
            pltpu.VMEM((2, C, rows, wc), f32),
            pltpu.VMEM((2, half, rows, wc), f32),
            pltpu.VMEM((2, half, rows, wc), f32),
            pltpu.VMEM((2, rows, wc), f32),
            pltpu.VMEM((2, C, span, wc), f32),
            pltpu.VMEM((3, W, wc), f32),
            pltpu.VMEM((3, g, W // g, wc), f32),
            pltpu.VMEM((3, W // g, wc), f32),
            pltpu.VMEM((3, C, W // R, wc), f32),
            pltpu.VMEM((C, 3 * W, wc), f32),
            pltpu.VMEM((W, W), f32),
            dma((4,)),
            dma((nsend,)),
            dma((2, C)),
            dma((2, g * C)),
            dma((2, C)),
            dma((2, half)),
            dma((2, half)),
            dma((2, C)),
            dma((3, g)),
            dma((3, C)),
            dma((3, C)),
            dma((3, g, half)),
            dma((3, g, half)),
            dma((3, g, half)),
        ]

    def paired(span, rows, K, W):
        wc, Z = W // C, R // 2
        nsend = 2 * (4 + 4 + 4 + 3 + 4) + 1 + 3 * (1 + 2 * (Z - 1) + 3 * Z + 4)
        return functools.partial(fast_body, R, C, nsend), [
            pltpu.VMEM((rows, K), f32),
            pltpu.VMEM((W, W), f32),
            pltpu.VMEM((W, W), f32),
            pltpu.VMEM((W, W), f32),
            pltpu.VMEM((2, K, W), f32),
            pltpu.VMEM((2, rows, W), f32),
            pltpu.VMEM((2, C, rows, wc), f32),
            pltpu.VMEM((2, 3, rows, wc), f32),
            pltpu.VMEM((2, rows, wc), f32),
            pltpu.VMEM((2, C, span, wc), f32),
            pltpu.VMEM((3, W, wc), f32),
            pltpu.VMEM((3, W // 2, wc), f32),
            pltpu.VMEM((3, W // 2, wc), f32),
            pltpu.VMEM((3, Z, W // R, wc), f32),
            pltpu.VMEM((C, 3 * W, wc), f32),
            pltpu.VMEM((W, W), f32),
            dma((3,)),
            dma((nsend,)),
            dma(()),
            dma((2, 2 * C)),
            dma((2, C)),
            dma((2, 3)),
            dma((2, C)),
            dma((3,)),
            dma((3, Z)),
            dma((3, Z)),
            dma((3, Z)),
            dma((3, Z)),
            dma((3, Z)),
            dma((3, 4)),
        ]

    def local(inverse_pool, panel_one, panel_two, upper_two, lower_one, lower_two, list_one, list_two):
        span, W = panel_one.shape
        rows, K = inverse_pool.shape
        kernel, scratch = (paired if (g, C) == (2, 4) else general)(span, rows, K, W)
        shapes = ((span, W), (W, W), (span, W), (W, W), (W, W))
        results = pl.pallas_call(
            kernel,
            out_shape=tuple(pltpu.VMEM(shape, f32) for shape in shapes),
            in_specs=[pl.BlockSpec(memory_space=pl.ANY)] * 6
            + [pl.BlockSpec(memory_space=pltpu.SMEM)] * 2,
            out_specs=(pl.BlockSpec(memory_space=pltpu.VMEM),) * 5,
            scratch_shapes=scratch,
            compiler_params=pltpu.CompilerParams(collective_id=0, has_side_effects=True),
        )(inverse_pool, panel_one, panel_two, upper_two, lower_one, lower_two, list_one, list_two)
        return pl.pallas_call(
            write_out,
            out_shape=tuple(jax.ShapeDtypeStruct(shape, f32) for shape in shapes),
            in_specs=[pl.BlockSpec(memory_space=pl.ANY)] * 5,
            out_specs=(pl.BlockSpec(memory_space=pl.ANY),) * 5,
            scratch_shapes=[dma((5,))],
            compiler_params=pltpu.CompilerParams(vmem_limit_bytes=8 * W * W * 4),
        )(*results)

    return jax.shard_map(
        local,
        mesh=mesh,
        in_specs=(
            P("prow", "pcol"),
            P(("prow", "pcol"), None),
            P(("prow", "pcol"), None),
            P(),
            P(),
            P(),
            P(),
            P(),
        ),
        out_specs=(P(("prow", "pcol"), None), P(), P(("prow", "pcol"), None), P(), P()),
        check_vma=False,
    )
```

```python
import functools

import jax
import jax.numpy as jnp
from jax import lax
from jax.experimental import pallas as pl
from jax.experimental.pallas import tpu as pltpu
from jax.sharding import PartitionSpec as P

BLK = 128
MESH = pl.DeviceIdType.MESH


def halves(value):
    high = value.astype(jnp.bfloat16)
    low = (value - high.astype(jnp.float32)).astype(jnp.bfloat16)
    return high, low


def split_dot(left, right, dims):
    def one(a, b):
        return lax.dot_general(a, b, (dims, ((), ())), preferred_element_type=jnp.float32)

    return one(left[0], right[0]) + (one(left[0], right[1]) + one(left[1], right[0]))


PLAIN = ((1,), (0,))
FIRST = ((0,), (0,))


def live_column(listing, first_row, count):
    blocks = (first_row + lax.broadcasted_iota(jnp.int32, (count, 1), 0)) // BLK

    def step(k, hits):
        return jnp.maximum(hits, jnp.where(blocks == listing[k], 1.0, 0.0).astype(jnp.float32))

    return lax.fori_loop(0, listing.shape[0], step, jnp.zeros((count, 1), jnp.float32))


def write_out(*refs):
    sems = refs[-1]
    copies = [pltpu.make_async_copy(refs[k], refs[5 + k], sems.at[k]) for k in range(5)]
    for copy in copies:
        copy.start()
    for copy in copies:
        copy.wait()


def body(
    R, C, nsend,
    x_in, one_in, two_in, u_in, l1_in, l2_in, list1, list2,
    f_out, d1_out, s_out, c_out, d2_out,
    x_v, u_v, l1_v, l2_v, zbuf, mcol, mrow, abuf, arecv, brecv, asum, frow, qbuf, xrecv, xsum, zrecv, qfull, wt,
    load_sem, send_sem, z_sem, m_sem, g_sem, a_sem, b_sem, f_sem, x_sem, q_sem, gz_sem, gx_sem, gy_sem, gc_sem,
):
    g, half = R // C, C // 2
    span, W = one_in.shape
    rows, K = x_in.shape
    wc = W // C
    part, ch = W // g, W // R
    p, c = lax.axis_index("prow"), lax.axis_index("pcol")
    z, i = p // g, p % g
    partner = c + 1 - 2 * (c % 2)
    panels = (one_in, two_in)
    pending = []

    def send(src, dst, recv_sem, to, when=None):
        copy = pltpu.make_async_remote_copy(
            src_ref=src, dst_ref=dst, send_sem=send_sem.at[len(pending)],
            recv_sem=recv_sem, device_id=to, device_id_type=MESH,
        )
        pending.append((copy, when))
        if when is None:
            copy.start()
        else:
            pl.when(when)(copy.start)

    def arrived(dst, recv_sem):
        pltpu.make_async_copy(dst, dst, recv_sem).wait()

    def at(base, index, size):
        return base.at[pl.ds(pl.multiple_of(index * size, 8), size)]

    def plane_peer(dz):
        return (((z + dz) % C) * g + i, c)

    def side_peer(di):
        return (z * g + (i + di) % g, c)

    loads = []
    for k, (src, dst) in enumerate(((l1_in, l1_v), (l2_in, l2_v), (x_in, x_v), (u_in, u_v))):
        copy = pltpu.make_async_copy(src, dst, load_sem.at[k])
        copy.start()
        loads.append(copy)

    barrier = pltpu.get_barrier_semaphore()
    peers = 0
    for dp in range(1, R):
        pl.semaphore_signal(barrier, inc=1, device_id=((p + dp) % R, c), device_id_type=MESH)
        peers += 1
    for di in range(g):
        for dc in range(1, C):
            pl.semaphore_signal(
                barrier, inc=1, device_id=(z * g + (i + di) % g, (c + dc) % C), device_id_type=MESH
            )
            peers += 1
    pl.semaphore_wait(barrier, peers)

    def to_columns(k, src, plane, valid=True):
        own = i * C + c
        dst, sem = at(mcol.at[k], own, span), m_sem.at[k, own]
        send(src, dst, sem, (p, plane), (plane != c) & valid)
        pl.when((plane == c) & valid)(pltpu.make_async_copy(src, dst, sem).start)
        for di in range(1, g):
            to = (z * g + (i + di) % g, plane)
            send(src, dst, sem, to, (plane // 2 == c // 2) & valid)

    def along(k, src, plane, way, valid=True):
        inside = (z + 1 < C) if way > 0 else (z > 0)
        send(src, zbuf.at[k, plane], z_sem.at[k, plane], plane_peer(way % C), inside & valid)

    def far(dy, parity):
        return ((c // 2 + dy) % half) * 2 + parity

    def across(k):
        for dy in range(1, half):
            for parity in range(2):
                slot = i * C + far(dy, parity)
                piece = at(mcol.at[k], slot, span)
                arrived(piece, m_sem.at[k, slot])
                for di in range(1, g):
                    send(piece, piece, m_sem.at[k, slot], side_peer(di))

    def columns_arrived(k):
        for dy in range(half):
            for parity in range(2):
                for di in range(1 if dy else 0, g):
                    slot = ((i + di) % g) * C + far(dy, parity)
                    arrived(at(mcol.at[k], slot, span), m_sem.at[k, slot])

    def to_row(k):
        dst, sem = at(mrow.at[k], c, span), g_sem.at[k, c]
        pltpu.make_async_copy(panels[k], dst, sem).start()
        for dc in range(2, C, 2):
            send(panels[k], dst, sem, (p, (c + dc) % C))
        send(panels[k], dst, sem, (p, partner))

    def row_onward(k):
        for dc in range(2, C, 2):
            other = (c + dc) % C
            piece = at(mrow.at[k], other, span)
            arrived(piece, g_sem.at[k, other])
            send(piece, piece, g_sem.at[k, other], (p, partner))

    def row_arrived(k):
        arrived(at(mrow.at[k], c, span), g_sem.at[k, c])
        for dc in range(0, C, 2):
            other = (partner + dc) % C
            arrived(at(mrow.at[k], other, span), g_sem.at[k, other])

    def tile_product(k, listing):
        columns_arrived(k)
        masked = live_column(listing, c * K, K) * mcol[k]
        product = split_dot(x_pair, halves(masked), PLAIN)
        for cc in range(C):
            abuf[k, cc] = product[:, cc * wc:(cc + 1) * wc]
        for j in range(half):
            send(abuf.at[k, (partner + 2 * j) % C], arecv.at[k, j], a_sem.at[k, j], (p, partner))

    def pair_sum(k):
        for j in list(range(1, half)) + [0]:
            other = (c + 2 * j) % C
            arrived(arecv.at[k, j], a_sem.at[k, j])
            abuf[k, other] = abuf[k, other] + arecv[k, j]
            if j:
                send(abuf.at[k, other], brecv.at[k, j], b_sem.at[k, j], (p, other))

    def total(k, mask):
        result = abuf[k, c]
        for j in range(1, half):
            arrived(brecv.at[k, j], b_sem.at[k, j])
            result = result + brecv[k, j]
        result = mask * result
        asum[k] = result
        return halves(result)

    def rows_out(k):
        for dc in range(1, C):
            other = (c + dc) % C
            send(at(asum.at[k], other, span), frow.at[k, c], f_sem.at[k, c], (p, other))
        frow[k, c] = asum[k, pl.ds(pl.multiple_of(c * span, 8), span)]

    def side_out(b):
        for di in range(1, g):
            other = (i + di) % g
            send(at(qbuf.at[b], other, part), xrecv.at[b, di], x_sem.at[b, di], side_peer(di))

    def side_in(b):
        result = qbuf[b, pl.ds(pl.multiple_of(i * part, 8), part)]
        for di in range(1, g):
            arrived(xrecv.at[b, di], x_sem.at[b, di])
            result = result + xrecv[b, di]
        xsum[b] = result
        for dz in range(1, C):
            send(at(xsum.at[b], (z + dz) % C, ch), zrecv.at[b, dz], q_sem.at[b, dz], plane_peer(dz))

    def block(b, column, side, plane):
        first = b * W + side * part + plane * ch
        return qfull.at[column, pl.ds(pl.multiple_of(first, 8), ch)]

    def block_part(b, column, side):
        return qfull.at[column, pl.ds(pl.multiple_of(b * W + side * part, 8), part)]

    def plane_in(b):
        result = xsum[b, pl.ds(pl.multiple_of(z * ch, 8), ch)]
        for dz in range(1, C):
            arrived(zrecv.at[b, dz], q_sem.at[b, dz])
            result = result + zrecv[b, dz]
        piece = block(b, c, i, z)
        piece[...] = result
        for dz in range(1, C):
            send(piece, piece, gz_sem.at[b, dz], plane_peer(dz))

    def gram_part(b, di, dc, base):
        return block_part(b, (base + C - dc) % C, (i + g - di) % g)

    def to_side(b, dc):
        piece = gram_part(b, 0, dc, c)
        for di in range(1, g):
            send(piece, piece, gx_sem.at[b, di, dc // 2], side_peer(di))

    def to_rows(b, di):
        piece = gram_part(b, di, 0, c)
        for dc in range(2, C, 2):
            send(piece, piece, gy_sem.at[b, di, dc // 2], (p, (c + dc) % C))

    def to_partner(b, di, dc):
        piece = gram_part(b, di, dc, c)
        send(piece, piece, gc_sem.at[b, di, dc // 2], (p, partner))

    def side_arrived(b, di, dc):
        arrived(gram_part(b, di, dc, c), gx_sem.at[b, di, dc // 2])

    def rows_arrived(b, di, dc):
        arrived(gram_part(b, di, dc, c), gy_sem.at[b, di, dc // 2])

    def gather_side(b):
        for dz in range(1, C):
            arrived(block(b, c, i, (z + C - dz) % C), gz_sem.at[b, dz])
        to_side(b, 0)
        to_rows(b, 0)
        to_partner(b, 0, 0)

    def gather_row(b):
        if b == 1:
            for dc in range(2, C, 2):
                rows_arrived(b, 0, dc)
                to_side(b, dc)
                to_partner(b, 0, dc)
        else:
            for di in range(1, g):
                side_arrived(b, di, 0)
                to_rows(b, di)
                to_partner(b, di, 0)

    def gather_core(b):
        if b == 1:
            for di in range(1, g):
                for dc in range(0, C, 2):
                    side_arrived(b, di, dc)
                    to_partner(b, di, dc)
        else:
            for di in range(g):
                for dc in range(2, C, 2):
                    rows_arrived(b, di, dc)
                    to_partner(b, di, dc)

    def gathered(b):
        for di in range(g):
            for dc in range(0, C, 2):
                piece = block_part(b, (partner + C - dc) % C, (i + g - di) % g)
                arrived(piece, gc_sem.at[b, di, dc // 2])

    for k in range(2):
        along(k, panels[k], z, 1)
        along(k, panels[k], z, -1)
        to_columns(k, panels[k], z)
    for k in range(2):
        for dz in range(1, C):
            for way in (1, -1):
                valid = (z >= dz) if way > 0 else (z + dz < C)
                plane = (z + C - way * dz) % C
                src, sem = zbuf.at[k, plane], z_sem.at[k, plane]
                pl.when(valid)(functools.partial(arrived, src, sem))
                if dz < C - 1:
                    along(k, src, plane, way, valid)
                to_columns(k, src, plane, valid)
        to_row(k)
        if k == 0:
            across(0)
            for copy in loads[2:]:
                copy.wait()
            x_pair = halves(x_v[...])
            row_one, row_two = live_column(list1, p * rows, rows), live_column(list2, p * rows, rows)
    row_onward(0)
    tile_product(0, list1)
    across(1)
    pair_sum(0)
    row_onward(1)
    row_arrived(0)
    left = halves(row_one * mrow[0])
    right_one = total(0, row_one)
    qbuf[0] = split_dot(left, right_one, FIRST)
    side_out(0)
    for copy in loads[:2]:
        copy.wait()
    for src, dst in ((l1_v, d1_out), (l2_v, d2_out)):
        pair = halves(src[...])
        dst[...] = split_dot(pair, pair, FIRST)
    tile_product(1, list2)
    pair_sum(1)
    row_arrived(1)
    left = halves(row_two * mrow[1])
    cross = split_dot(right_one, left, FIRST)
    for cc in range(C):
        qbuf[1, cc * wc:(cc + 1) * wc] = cross[:, cc * wc:(cc + 1) * wc]
    side_out(1)
    side_in(0)
    right_two = total(1, row_two)
    qbuf[2] = split_dot(left, right_two, FIRST)
    side_out(2)
    plane_in(0)
    side_in(1)
    gather_side(0)
    plane_in(1)
    side_in(2)
    gather_row(0)
    gather_side(1)
    plane_in(2)
    gather_core(0)
    gather_row(1)
    gather_side(2)
    rows_out(0)
    rows_out(1)
    gather_core(1)
    gather_row(2)

    u_pair = halves(u_v[...])
    gathered(0)
    for cc in range(C):
        d1_out[:, cc * wc:(cc + 1) * wc] += qfull[cc, 0:W]
    d1_u = split_dot(halves(d1_out[...]), u_pair, PLAIN)
    gather_core(2)
    for k in range(2):
        for dc in range(1, C):
            other = (c + dc) % C
            arrived(frow.at[k, other], f_sem.at[k, other])
    for cc in range(C):
        f_out[:, cc * wc:(cc + 1) * wc] = -frow[0, cc]
        s_out[:, cc * wc:(cc + 1) * wc] = frow[1, cc]
    f_u = split_dot(halves(f_out[...]), u_pair, PLAIN)
    s_out[...] = -live_column(list2, p * rows + c * span, span) * (f_u + s_out[...])

    gathered(1)
    for cc in range(C):
        for k in range(C):
            wt[cc * wc:(cc + 1) * wc, k * wc:(k + 1) * wc] = qfull[cc, W + k * wc:W + (k + 1) * wc]
    c_out[...] = wt[...] - d1_u
    d2_out[...] -= split_dot(u_pair, halves(c_out[...]), FIRST) + split_dot(
        halves(wt[...]), u_pair, FIRST
    )
    gathered(2)
    for cc in range(C):
        d2_out[:, cc * wc:(cc + 1) * wc] += qfull[cc, 2 * W:3 * W]

    assert len(pending) <= nsend
    for copy, when in pending:
        if when is None:
            copy.wait_send()
        else:
            pl.when(when)(copy.wait_send)


def fast_body(
    R, C, nsend,
    x_in, one_in, two_in, u_in, l1_in, l2_in, list1, list2,
    f_out, d1_out, s_out, c_out, d2_out,
    x_v, u_v, l1_v, l2_v, mcol, mrow, abuf, arecv, asum, frow, qbuf, krecv, ksum, zrecv, qfull, wt,
    load_sem, send_sem, x_sem, m_sem, g_sem, a_sem, f_sem, k_sem, q_sem, gz_sem, gx_sem, gy_sem, gd_sem, gc_sem,
):
    span, W = one_in.shape
    rows, K = x_in.shape
    wc = W // C
    Z = R // 2
    part, ch = W // 2, W // R
    p, c = lax.axis_index("prow"), lax.axis_index("pcol")
    z, x, y, k = p // 2, p % 2, c // 2, c % 2
    slab = 2 * y + x
    panels = (one_in, two_in)
    others = ((1, 0), (0, 1), (1, 1))
    pending = []

    def dev(x, y, z, k):
        return (z * 2 + x, y * 2 + k)

    def send(src, dst, recv_sem, to, when=None):
        copy = pltpu.make_async_remote_copy(
            src_ref=src, dst_ref=dst, send_sem=send_sem.at[len(pending)],
            recv_sem=recv_sem, device_id=to, device_id_type=MESH,
        )
        pending.append((copy, when))
        if when is None:
            copy.start()
        else:
            pl.when(when)(copy.start)

    def arrived(dst, recv_sem):
        pltpu.make_async_copy(dst, dst, recv_sem).wait()

    def at(base, index, size):
        return base.at[pl.ds(pl.multiple_of(index * size, 8), size)]

    def send_or_copy(src, dst, sem, to, here):
        send(src, dst, sem, to, jnp.logical_not(here))
        pl.when(here)(pltpu.make_async_copy(src, dst, sem).start)

    pl.when(k == x)(pltpu.make_async_copy(x_in, x_v, x_sem).start)
    loads = []
    for n, (src, dst) in enumerate(((l1_in, l1_v), (l2_in, l2_v), (u_in, u_v))):
        copy = pltpu.make_async_copy(src, dst, load_sem.at[n])
        copy.start()
        loads.append(copy)

    barrier = pltpu.get_barrier_semaphore()

    def greet(to):
        pl.semaphore_signal(barrier, inc=1, device_id=to, device_id_type=MESH)

    @pl.when(slab != z)
    def _():
        for sx in range(2):
            for sy in range(2):
                greet(dev(sx, sy, slab, k))

    for dz in range(1, Z):
        greet(dev(x, y, (z + dz) % Z, k))
    for d in range(1, 8):
        greet(dev((x + d % 2) % 2, (y + d // 2 % 2) % 2, z, (k + d // 4) % 2))
    pl.semaphore_wait(barrier, 7 + 2 * (Z - 1))

    own = x * C + c

    def in_columns(b, slot):
        return at(mcol.at[b], slot, span), m_sem.at[b, slot]

    def panel_out(b):
        px, py = z % 2, z // 2
        dst, sem = in_columns(b, own)
        for dz in (2, 3, 1):
            send(panels[b], dst, sem, dev(px, py, (z + dz) % Z, k))
        send_or_copy(panels[b], dst, sem, dev(px, py, z, k), (x == px) & (y == py))

    def left_out(b):
        dst, sem = at(mrow.at[b], c, span), g_sem.at[b, c]
        for dx, dy in others:
            send(panels[b], dst, sem, dev((x + dx) % 2, (y + dy) % 2, z, x))
        send_or_copy(panels[b], dst, sem, dev(x, y, z, 1 - k), k == x)

    def columns_in(b):
        for sx in range(2):
            for sy in range(2):
                piece, sem = in_columns(b, sx * C + 2 * sy + k)
                arrived(piece, sem)
                send(piece, piece, sem, dev(x, y, z, 1 - k))

    def columns_arrived(b):
        for sx in range(2):
            for sy in range(2):
                arrived(*in_columns(b, sx * C + 2 * sy + 1 - k))

    def left_arrived(b):
        for n in range(C):
            arrived(at(mrow.at[b], n, span), g_sem.at[b, n])

    def tile_product(b, listing):
        live = live_column(listing, slab * K, K)
        for dy in (1, 0):
            ty = (y + dy) % 2
            columns = pl.ds(pl.multiple_of(ty * 2 * wc, 2 * wc), 2 * wc)
            product = split_dot(x_pair, halves(live * mcol[b, :, columns]), PLAIN)
            for n in range(2):
                abuf[b, 2 * ty + n] = product[:, n * wc:(n + 1) * wc]
            for n, (dx, my) in enumerate(others):
                if my == dy:
                    tx = (x + dx) % 2
                    send(abuf.at[b, 2 * ty + tx], arecv.at[b, n], a_sem.at[b, n], dev(tx, ty, z, k))

    def total(b, mask):
        result = abuf[b, slab]
        for n in range(len(others)):
            arrived(arecv.at[b, n], a_sem.at[b, n])
            result = result + arecv[b, n]
        result = mask * result
        asum[b] = result
        return halves(result)

    def rows_out(b):
        for dy in range(2):
            for dk in range(2):
                ty, tk = (y + dy) % 2, (k + dk) % 2
                src, dst, sem = at(asum.at[b], 2 * ty + tk, span), frow.at[b, slab], f_sem.at[b, slab]
                if dy or dk:
                    send(src, dst, sem, dev(k, ty, z, tk))
                else:
                    send_or_copy(src, dst, sem, dev(k, ty, z, tk), k == x)

    def core_out(b):
        send(at(qbuf.at[b], 1 - k, part), krecv.at[b], k_sem.at[b], dev(x, y, z, 1 - k))

    def core_in(b):
        arrived(krecv.at[b], k_sem.at[b])
        ksum[b] = qbuf[b, pl.ds(pl.multiple_of(k * part, 8), part)] + krecv[b]
        for dz in range(1, Z):
            to = (z + dz) % Z
            send(at(ksum.at[b], to, ch), zrecv.at[b, dz], q_sem.at[b, dz], dev(x, y, to, k))

    def region(b, column, core):
        return qfull.at[column, pl.ds(pl.multiple_of(b * W + core * part, 8), part)]

    def chunk(b, column, core, dz):
        plane = (z + Z - dz) % Z
        return qfull.at[column, pl.ds(pl.multiple_of(b * W + core * part + plane * ch, 8), ch)]

    beside, along, across = 2 * y + 1 - x, 2 * (1 - y) + x, 2 * (1 - y) + 1 - x

    def to_core(piece, sem):
        send(piece, piece, sem, dev(x, y, z, 1 - k))

    def to_near(b, dz):
        piece = chunk(b, slab, k, dz)
        send(piece, piece, gx_sem.at[b, dz], dev(1 - x, y, z, k))
        send(piece, piece, gy_sem.at[b, dz], dev(x, 1 - y, z, k))

    def planes_in(b):
        result = ksum[b, pl.ds(pl.multiple_of(z * ch, 8), ch)]
        for dz in range(1, Z):
            arrived(zrecv.at[b, dz], q_sem.at[b, dz])
            result = result + zrecv[b, dz]
        piece = chunk(b, slab, k, 0)
        piece[...] = result
        for dz in range(1, Z):
            send(piece, piece, gz_sem.at[b, dz], dev(x, y, (z + dz) % Z, k))
        to_near(b, 0)

    def planes_on(b):
        for dz in range(1, Z):
            arrived(chunk(b, slab, k, dz), gz_sem.at[b, dz])
            to_near(b, dz)
        to_core(region(b, slab, k), gc_sem.at[b, 0])

    def near_on(b, dz):
        piece = chunk(b, beside, k, dz)
        arrived(piece, gx_sem.at[b, dz])
        if dz % 2 == 0:
            send(piece, piece, gd_sem.at[b, dz], dev(x, 1 - y, z, k))
        piece = chunk(b, along, k, dz)
        arrived(piece, gy_sem.at[b, dz])
        if dz % 2 == 1:
            send(piece, piece, gd_sem.at[b, dz], dev(1 - x, y, z, k))

    def near_rest(b):
        for dz in range(1, Z):
            near_on(b, dz)
        to_core(region(b, beside, k), gc_sem.at[b, 1])
        to_core(region(b, along, k), gc_sem.at[b, 2])

    def gather_far(b):
        for dz in range(Z):
            arrived(chunk(b, across, k, dz), gd_sem.at[b, dz])
        to_core(region(b, across, k), gc_sem.at[b, 3])

    def gathered(b):
        for n, column in enumerate((slab, beside, along, across)):
            arrived(region(b, column, 1 - k), gc_sem.at[b, n])

    def square(n, src, dst):
        loads[n].wait()
        pair = halves(src[...])
        dst[...] = split_dot(pair, pair, FIRST)

    panel_out(0)
    send(x_in, x_v, x_sem, dev(1 - x, y, z, 1 - k), k != x)
    panel_out(1)
    left_out(0)
    square(0, l1_v, d1_out)
    square(1, l2_v, d2_out)
    block_row = 2 * z + k
    row_one, row_two = live_column(list1, block_row * rows, rows), live_column(list2, block_row * rows, rows)
    arrived(x_v, x_sem)
    x_pair = halves(x_v[...])
    columns_in(0)
    columns_arrived(0)
    tile_product(0, list1)
    left_out(1)
    left_arrived(0)
    left_one = halves(row_one * mrow[0])
    loads[2].wait()
    u_pair = halves(u_v[...])
    columns_in(1)
    right_one = total(0, row_one)
    qbuf[0] = split_dot(left_one, right_one, FIRST)
    core_out(0)
    rows_out(0)
    core_in(0)
    columns_arrived(1)
    tile_product(1, list2)
    left_arrived(1)
    left_two = halves(row_two * mrow[1])
    cross = split_dot(right_one, left_two, FIRST)
    for n in range(C):
        qbuf[1, n * wc:(n + 1) * wc] = cross[:, n * wc:(n + 1) * wc]
    core_out(1)
    planes_in(0)
    core_in(1)
    right_two = total(1, row_two)
    qbuf[2] = split_dot(left_two, right_two, FIRST)
    core_out(2)
    rows_out(1)
    planes_in(1)
    planes_on(0)
    core_in(2)
    near_on(0, 0)
    planes_on(1)
    near_rest(0)
    planes_in(2)
    near_on(1, 0)
    near_rest(1)
    gather_far(0)
    for b in range(2):
        for n in range(C):
            arrived(frow.at[b, n], f_sem.at[b, n])
    for n in range(C):
        f_out[:, n * wc:(n + 1) * wc] = -frow[0, n]
        s_out[:, n * wc:(n + 1) * wc] = frow[1, n]
    f_u = split_dot(halves(f_out[...]), u_pair, PLAIN)
    s_out[...] = -live_column(list2, p * rows + c * span, span) * (f_u + s_out[...])
    planes_on(2)
    near_on(2, 0)
    gathered(0)
    for n in range(C):
        d1_out[:, n * wc:(n + 1) * wc] += qfull[n, 0:W]
    d1_u = split_dot(halves(d1_out[...]), u_pair, PLAIN)
    gather_far(1)
    near_rest(2)
    gathered(1)
    for n in range(C):
        for m in range(C):
            wt[n * wc:(n + 1) * wc, m * wc:(m + 1) * wc] = qfull[n, W + m * wc:W + (m + 1) * wc]
    c_out[...] = wt[...] - d1_u
    d2_out[...] -= split_dot(u_pair, halves(c_out[...]), FIRST) + split_dot(
        halves(wt[...]), u_pair, FIRST
    )
    gather_far(2)
    gathered(2)
    for n in range(C):
        d2_out[:, n * wc:(n + 1) * wc] += qfull[n, 2 * W:3 * W]

    assert len(pending) <= nsend
    for copy, when in pending:
        if when is None:
            copy.wait_send()
        else:
            pl.when(when)(copy.wait_send)


def solution(mesh):
    R, C = mesh.shape["prow"], mesh.shape["pcol"]
    g = R // C
    f32, dma = jnp.float32, pltpu.SemaphoreType.DMA

    def general(span, rows, K, W):
        wc, half = W // C, C // 2
        panel = 2 * (C - 1) + (2 * C - 1) * g + 2 * (half - 1) * (g - 1) + half + (half - 1)
        reduced = half + (half - 1) + (C - 1)
        gram = (g - 1) + 2 * (C - 1) + (g - 1) + g * half + g * (half - 1)
        nsend = 2 * panel + 2 * reduced + 3 * gram
        return functools.partial(body, R, C, nsend), [
            pltpu.VMEM((rows, K), f32),
            pltpu.VMEM((W, W), f32),
            pltpu.VMEM((W, W), f32),
            pltpu.VMEM((W, W), f32),
            pltpu.VMEM((2, C, span, W), f32),
            pltpu.VMEM((2, K, W), f32),
            pltpu.VMEM((2, rows, W), f32),
            pltpu.VMEM((2, C, rows, wc), f32),
            pltpu.VMEM((2, half, rows, wc), f32),
            pltpu.VMEM((2, half, rows, wc), f32),
            pltpu.VMEM((2, rows, wc), f32),
            pltpu.VMEM((2, C, span, wc), f32),
            pltpu.VMEM((3, W, wc), f32),
            pltpu.VMEM((3, g, W // g, wc), f32),
            pltpu.VMEM((3, W // g, wc), f32),
            pltpu.VMEM((3, C, W // R, wc), f32),
            pltpu.VMEM((C, 3 * W, wc), f32),
            pltpu.VMEM((W, W), f32),
            dma((4,)),
            dma((nsend,)),
            dma((2, C)),
            dma((2, g * C)),
            dma((2, C)),
            dma((2, half)),
            dma((2, half)),
            dma((2, C)),
            dma((3, g)),
            dma((3, C)),
            dma((3, C)),
            dma((3, g, half)),
            dma((3, g, half)),
            dma((3, g, half)),
        ]

    def paired(span, rows, K, W):
        wc, Z = W // C, R // 2
        nsend = 2 * (4 + 4 + 4 + 3 + 4) + 1 + 3 * (1 + 2 * (Z - 1) + 3 * Z + 4)
        return functools.partial(fast_body, R, C, nsend), [
            pltpu.VMEM((rows, K), f32),
            pltpu.VMEM((W, W), f32),
            pltpu.VMEM((W, W), f32),
            pltpu.VMEM((W, W), f32),
            pltpu.VMEM((2, K, W), f32),
            pltpu.VMEM((2, rows, W), f32),
            pltpu.VMEM((2, C, rows, wc), f32),
            pltpu.VMEM((2, 3, rows, wc), f32),
            pltpu.VMEM((2, rows, wc), f32),
            pltpu.VMEM((2, C, span, wc), f32),
            pltpu.VMEM((3, W, wc), f32),
            pltpu.VMEM((3, W // 2, wc), f32),
            pltpu.VMEM((3, W // 2, wc), f32),
            pltpu.VMEM((3, Z, W // R, wc), f32),
            pltpu.VMEM((C, 3 * W, wc), f32),
            pltpu.VMEM((W, W), f32),
            dma((3,)),
            dma((nsend,)),
            dma(()),
            dma((2, 2 * C)),
            dma((2, C)),
            dma((2, 3)),
            dma((2, C)),
            dma((3,)),
            dma((3, Z)),
            dma((3, Z)),
            dma((3, Z)),
            dma((3, Z)),
            dma((3, Z)),
            dma((3, 4)),
        ]

    def local(inverse_pool, panel_one, panel_two, upper_two, lower_one, lower_two, list_one, list_two):
        span, W = panel_one.shape
        rows, K = inverse_pool.shape
        kernel, scratch = (paired if (g, C) == (2, 4) else general)(span, rows, K, W)
        shapes = ((span, W), (W, W), (span, W), (W, W), (W, W))
        results = pl.pallas_call(
            kernel,
            out_shape=tuple(pltpu.VMEM(shape, f32) for shape in shapes),
            in_specs=[pl.BlockSpec(memory_space=pl.ANY)] * 6
            + [pl.BlockSpec(memory_space=pltpu.SMEM)] * 2,
            out_specs=(pl.BlockSpec(memory_space=pltpu.VMEM),) * 5,
            scratch_shapes=scratch,
            compiler_params=pltpu.CompilerParams(collective_id=0, has_side_effects=True),
        )(inverse_pool, panel_one, panel_two, upper_two, lower_one, lower_two, list_one, list_two)
        return pl.pallas_call(
            write_out,
            out_shape=tuple(jax.ShapeDtypeStruct(shape, f32) for shape in shapes),
            in_specs=[pl.BlockSpec(memory_space=pl.ANY)] * 5,
            out_specs=(pl.BlockSpec(memory_space=pl.ANY),) * 5,
            scratch_shapes=[dma((5,))],
            compiler_params=pltpu.CompilerParams(vmem_limit_bytes=8 * W * W * 4),
        )(*results)

    return jax.shard_map(
        local,
        mesh=mesh,
        in_specs=(
            P("prow", "pcol"),
            P(("prow", "pcol"), None),
            P(("prow", "pcol"), None),
            P(),
            P(),
            P(),
            P(),
            P(),
        ),
        out_specs=(P(("prow", "pcol"), None), P(), P(("prow", "pcol"), None), P(), P()),
        check_vma=False,
    )
```

```python
import functools

import jax
import jax.numpy as jnp
from jax import lax
from jax.experimental import pallas as pl
from jax.experimental.pallas import tpu as pltpu
from jax.sharding import PartitionSpec as P

BLK = 128
MESH = pl.DeviceIdType.MESH


def halves(value):
    high = value.astype(jnp.bfloat16)
    low = (value - high.astype(jnp.float32)).astype(jnp.bfloat16)
    return high, low


def split_dot(left, right, dims):
    def one(a, b):
        return lax.dot_general(a, b, (dims, ((), ())), preferred_element_type=jnp.float32)

    return one(left[0], right[0]) + (one(left[0], right[1]) + one(left[1], right[0]))


PLAIN = ((1,), (0,))
FIRST = ((0,), (0,))


def live_column(listing, first_row, count):
    blocks = (first_row + lax.broadcasted_iota(jnp.int32, (count, 1), 0)) // BLK

    def step(k, hits):
        return jnp.maximum(hits, jnp.where(blocks == listing[k], 1.0, 0.0).astype(jnp.float32))

    return lax.fori_loop(0, listing.shape[0], step, jnp.zeros((count, 1), jnp.float32))


def write_out(*refs):
    sems = refs[-1]
    copies = [pltpu.make_async_copy(refs[k], refs[5 + k], sems.at[k]) for k in range(5)]
    for copy in copies:
        copy.start()
    for copy in copies:
        copy.wait()


def body(
    R, C, nsend,
    x_in, one_in, two_in, u_in, l1_in, l2_in, list1, list2,
    f_out, d1_out, s_out, c_out, d2_out,
    x_v, u_v, l1_v, l2_v, zbuf, mcol, mrow, abuf, arecv, brecv, asum, frow, qbuf, xrecv, xsum, zrecv, qfull, wt,
    load_sem, send_sem, z_sem, m_sem, g_sem, a_sem, b_sem, f_sem, x_sem, q_sem, gz_sem, gx_sem, gy_sem, gc_sem,
):
    g, half = R // C, C // 2
    span, W = one_in.shape
    rows, K = x_in.shape
    wc = W // C
    part, ch = W // g, W // R
    p, c = lax.axis_index("prow"), lax.axis_index("pcol")
    z, i = p // g, p % g
    partner = c + 1 - 2 * (c % 2)
    panels = (one_in, two_in)
    pending = []

    def send(src, dst, recv_sem, to, when=None):
        copy = pltpu.make_async_remote_copy(
            src_ref=src, dst_ref=dst, send_sem=send_sem.at[len(pending)],
            recv_sem=recv_sem, device_id=to, device_id_type=MESH,
        )
        pending.append((copy, when))
        if when is None:
            copy.start()
        else:
            pl.when(when)(copy.start)

    def arrived(dst, recv_sem):
        pltpu.make_async_copy(dst, dst, recv_sem).wait()

    def at(base, index, size):
        return base.at[pl.ds(pl.multiple_of(index * size, 8), size)]

    def plane_peer(dz):
        return (((z + dz) % C) * g + i, c)

    def side_peer(di):
        return (z * g + (i + di) % g, c)

    loads = []
    for k, (src, dst) in enumerate(((l1_in, l1_v), (l2_in, l2_v), (x_in, x_v), (u_in, u_v))):
        copy = pltpu.make_async_copy(src, dst, load_sem.at[k])
        copy.start()
        loads.append(copy)

    barrier = pltpu.get_barrier_semaphore()
    peers = 0
    for dp in range(1, R):
        pl.semaphore_signal(barrier, inc=1, device_id=((p + dp) % R, c), device_id_type=MESH)
        peers += 1
    for di in range(g):
        for dc in range(1, C):
            pl.semaphore_signal(
                barrier, inc=1, device_id=(z * g + (i + di) % g, (c + dc) % C), device_id_type=MESH
            )
            peers += 1
    pl.semaphore_wait(barrier, peers)

    def to_columns(k, src, plane, valid=True):
        own = i * C + c
        dst, sem = at(mcol.at[k], own, span), m_sem.at[k, own]
        send(src, dst, sem, (p, plane), (plane != c) & valid)
        pl.when((plane == c) & valid)(pltpu.make_async_copy(src, dst, sem).start)
        for di in range(1, g):
            to = (z * g + (i + di) % g, plane)
            send(src, dst, sem, to, (plane // 2 == c // 2) & valid)

    def along(k, src, plane, way, valid=True):
        inside = (z + 1 < C) if way > 0 else (z > 0)
        send(src, zbuf.at[k, plane], z_sem.at[k, plane], plane_peer(way % C), inside & valid)

    def far(dy, parity):
        return ((c // 2 + dy) % half) * 2 + parity

    def across(k):
        for dy in range(1, half):
            for parity in range(2):
                slot = i * C + far(dy, parity)
                piece = at(mcol.at[k], slot, span)
                arrived(piece, m_sem.at[k, slot])
                for di in range(1, g):
                    send(piece, piece, m_sem.at[k, slot], side_peer(di))

    def columns_arrived(k):
        for dy in range(half):
            for parity in range(2):
                for di in range(1 if dy else 0, g):
                    slot = ((i + di) % g) * C + far(dy, parity)
                    arrived(at(mcol.at[k], slot, span), m_sem.at[k, slot])

    def to_row(k):
        dst, sem = at(mrow.at[k], c, span), g_sem.at[k, c]
        pltpu.make_async_copy(panels[k], dst, sem).start()
        for dc in range(2, C, 2):
            send(panels[k], dst, sem, (p, (c + dc) % C))
        send(panels[k], dst, sem, (p, partner))

    def row_onward(k):
        for dc in range(2, C, 2):
            other = (c + dc) % C
            piece = at(mrow.at[k], other, span)
            arrived(piece, g_sem.at[k, other])
            send(piece, piece, g_sem.at[k, other], (p, partner))

    def row_arrived(k):
        arrived(at(mrow.at[k], c, span), g_sem.at[k, c])
        for dc in range(0, C, 2):
            other = (partner + dc) % C
            arrived(at(mrow.at[k], other, span), g_sem.at[k, other])

    def tile_product(k, listing):
        columns_arrived(k)
        masked = live_column(listing, c * K, K) * mcol[k]
        product = split_dot(x_pair, halves(masked), PLAIN)
        for cc in range(C):
            abuf[k, cc] = product[:, cc * wc:(cc + 1) * wc]
        for j in range(half):
            send(abuf.at[k, (partner + 2 * j) % C], arecv.at[k, j], a_sem.at[k, j], (p, partner))

    def pair_sum(k):
        for j in list(range(1, half)) + [0]:
            other = (c + 2 * j) % C
            arrived(arecv.at[k, j], a_sem.at[k, j])
            abuf[k, other] = abuf[k, other] + arecv[k, j]
            if j:
                send(abuf.at[k, other], brecv.at[k, j], b_sem.at[k, j], (p, other))

    def total(k, mask):
        result = abuf[k, c]
        for j in range(1, half):
            arrived(brecv.at[k, j], b_sem.at[k, j])
            result = result + brecv[k, j]
        result = mask * result
        asum[k] = result
        return halves(result)

    def rows_out(k):
        for dc in range(1, C):
            other = (c + dc) % C
            send(at(asum.at[k], other, span), frow.at[k, c], f_sem.at[k, c], (p, other))
        frow[k, c] = asum[k, pl.ds(pl.multiple_of(c * span, 8), span)]

    def side_out(b):
        for di in range(1, g):
            other = (i + di) % g
            send(at(qbuf.at[b], other, part), xrecv.at[b, di], x_sem.at[b, di], side_peer(di))

    def side_in(b):
        result = qbuf[b, pl.ds(pl.multiple_of(i * part, 8), part)]
        for di in range(1, g):
            arrived(xrecv.at[b, di], x_sem.at[b, di])
            result = result + xrecv[b, di]
        xsum[b] = result
        for dz in range(1, C):
            send(at(xsum.at[b], (z + dz) % C, ch), zrecv.at[b, dz], q_sem.at[b, dz], plane_peer(dz))

    def block(b, column, side, plane):
        first = b * W + side * part + plane * ch
        return qfull.at[column, pl.ds(pl.multiple_of(first, 8), ch)]

    def block_part(b, column, side):
        return qfull.at[column, pl.ds(pl.multiple_of(b * W + side * part, 8), part)]

    def plane_in(b):
        result = xsum[b, pl.ds(pl.multiple_of(z * ch, 8), ch)]
        for dz in range(1, C):
            arrived(zrecv.at[b, dz], q_sem.at[b, dz])
            result = result + zrecv[b, dz]
        piece = block(b, c, i, z)
        piece[...] = result
        for dz in range(1, C):
            send(piece, piece, gz_sem.at[b, dz], plane_peer(dz))

    def gram_part(b, di, dc, base):
        return block_part(b, (base + C - dc) % C, (i + g - di) % g)

    def to_side(b, dc):
        piece = gram_part(b, 0, dc, c)
        for di in range(1, g):
            send(piece, piece, gx_sem.at[b, di, dc // 2], side_peer(di))

    def to_rows(b, di):
        piece = gram_part(b, di, 0, c)
        for dc in range(2, C, 2):
            send(piece, piece, gy_sem.at[b, di, dc // 2], (p, (c + dc) % C))

    def to_partner(b, di, dc):
        piece = gram_part(b, di, dc, c)
        send(piece, piece, gc_sem.at[b, di, dc // 2], (p, partner))

    def side_arrived(b, di, dc):
        arrived(gram_part(b, di, dc, c), gx_sem.at[b, di, dc // 2])

    def rows_arrived(b, di, dc):
        arrived(gram_part(b, di, dc, c), gy_sem.at[b, di, dc // 2])

    def gather_side(b):
        for dz in range(1, C):
            arrived(block(b, c, i, (z + C - dz) % C), gz_sem.at[b, dz])
        to_side(b, 0)
        to_rows(b, 0)
        to_partner(b, 0, 0)

    def gather_row(b):
        if b == 1:
            for dc in range(2, C, 2):
                rows_arrived(b, 0, dc)
                to_side(b, dc)
                to_partner(b, 0, dc)
        else:
            for di in range(1, g):
                side_arrived(b, di, 0)
                to_rows(b, di)
                to_partner(b, di, 0)

    def gather_core(b):
        if b == 1:
            for di in range(1, g):
                for dc in range(0, C, 2):
                    side_arrived(b, di, dc)
                    to_partner(b, di, dc)
        else:
            for di in range(g):
                for dc in range(2, C, 2):
                    rows_arrived(b, di, dc)
                    to_partner(b, di, dc)

    def gathered(b):
        for di in range(g):
            for dc in range(0, C, 2):
                piece = block_part(b, (partner + C - dc) % C, (i + g - di) % g)
                arrived(piece, gc_sem.at[b, di, dc // 2])

    for k in range(2):
        along(k, panels[k], z, 1)
        along(k, panels[k], z, -1)
        to_columns(k, panels[k], z)
    for k in range(2):
        for dz in range(1, C):
            for way in (1, -1):
                valid = (z >= dz) if way > 0 else (z + dz < C)
                plane = (z + C - way * dz) % C
                src, sem = zbuf.at[k, plane], z_sem.at[k, plane]
                pl.when(valid)(functools.partial(arrived, src, sem))
                if dz < C - 1:
                    along(k, src, plane, way, valid)
                to_columns(k, src, plane, valid)
        to_row(k)
        if k == 0:
            across(0)
            for copy in loads[2:]:
                copy.wait()
            x_pair = halves(x_v[...])
            row_one, row_two = live_column(list1, p * rows, rows), live_column(list2, p * rows, rows)
    row_onward(0)
    tile_product(0, list1)
    across(1)
    pair_sum(0)
    row_onward(1)
    row_arrived(0)
    left = halves(row_one * mrow[0])
    right_one = total(0, row_one)
    qbuf[0] = split_dot(left, right_one, FIRST)
    side_out(0)
    for copy in loads[:2]:
        copy.wait()
    for src, dst in ((l1_v, d1_out), (l2_v, d2_out)):
        pair = halves(src[...])
        dst[...] = split_dot(pair, pair, FIRST)
    tile_product(1, list2)
    pair_sum(1)
    row_arrived(1)
    left = halves(row_two * mrow[1])
    cross = split_dot(right_one, left, FIRST)
    for cc in range(C):
        qbuf[1, cc * wc:(cc + 1) * wc] = cross[:, cc * wc:(cc + 1) * wc]
    side_out(1)
    side_in(0)
    right_two = total(1, row_two)
    qbuf[2] = split_dot(left, right_two, FIRST)
    side_out(2)
    plane_in(0)
    side_in(1)
    gather_side(0)
    plane_in(1)
    side_in(2)
    gather_row(0)
    gather_side(1)
    plane_in(2)
    gather_core(0)
    gather_row(1)
    gather_side(2)
    rows_out(0)
    rows_out(1)
    gather_core(1)
    gather_row(2)

    u_pair = halves(u_v[...])
    gathered(0)
    for cc in range(C):
        d1_out[:, cc * wc:(cc + 1) * wc] += qfull[cc, 0:W]
    d1_u = split_dot(halves(d1_out[...]), u_pair, PLAIN)
    gather_core(2)
    for k in range(2):
        for dc in range(1, C):
            other = (c + dc) % C
            arrived(frow.at[k, other], f_sem.at[k, other])
    for cc in range(C):
        f_out[:, cc * wc:(cc + 1) * wc] = -frow[0, cc]
        s_out[:, cc * wc:(cc + 1) * wc] = frow[1, cc]
    f_u = split_dot(halves(f_out[...]), u_pair, PLAIN)
    s_out[...] = -live_column(list2, p * rows + c * span, span) * (f_u + s_out[...])

    gathered(1)
    for cc in range(C):
        for k in range(C):
            wt[cc * wc:(cc + 1) * wc, k * wc:(k + 1) * wc] = qfull[cc, W + k * wc:W + (k + 1) * wc]
    c_out[...] = wt[...] - d1_u
    d2_out[...] -= split_dot(u_pair, halves(c_out[...]), FIRST) + split_dot(
        halves(wt[...]), u_pair, FIRST
    )
    gathered(2)
    for cc in range(C):
        d2_out[:, cc * wc:(cc + 1) * wc] += qfull[cc, 2 * W:3 * W]

    assert len(pending) <= nsend
    for copy, when in pending:
        if when is None:
            copy.wait_send()
        else:
            pl.when(when)(copy.wait_send)


def fast_body(
    R, C, nsend,
    x_in, one_in, two_in, u_in, l1_in, l2_in, list1, list2,
    f_out, d1_out, s_out, c_out, d2_out,
    x_v, u_v, l1_v, l2_v, panels, mcol, mrow, abuf, arecv, asum, frow, qbuf, krecv, ksum, zrecv, qfull, wt,
    load_sem, send_sem, x_sem, m_sem, g_sem, a_sem, f_sem, k_sem, q_sem, gz_sem, gx_sem, gy_sem, gd_sem, gc_sem,
):
    span, W = one_in.shape
    rows, K = x_in.shape
    wc = W // C
    Z = R // 2
    part, ch = W // 2, W // R
    p, c = lax.axis_index("prow"), lax.axis_index("pcol")
    z, x, y, k = p // 2, p % 2, c // 2, c % 2
    slab = 2 * y + x
    others = ((1, 0), (0, 1), (1, 1))
    pending = []

    def dev(x, y, z, k):
        return (z * 2 + x, y * 2 + k)

    def send(src, dst, recv_sem, to, when=None):
        copy = pltpu.make_async_remote_copy(
            src_ref=src, dst_ref=dst, send_sem=send_sem.at[len(pending)],
            recv_sem=recv_sem, device_id=to, device_id_type=MESH,
        )
        pending.append((copy, when))
        if when is None:
            copy.start()
        else:
            pl.when(when)(copy.start)

    def arrived(dst, recv_sem):
        pltpu.make_async_copy(dst, dst, recv_sem).wait()

    def at(base, index, size):
        return base.at[pl.ds(pl.multiple_of(index * size, 8), size)]

    def send_or_copy(src, dst, sem, to, here):
        send(src, dst, sem, to, jnp.logical_not(here))
        pl.when(here)(pltpu.make_async_copy(src, dst, sem).start)

    pl.when(k == x)(pltpu.make_async_copy(x_in, x_v, x_sem).start)
    staged = []
    for n, src in enumerate((one_in, two_in)):
        copy = pltpu.make_async_copy(src, panels.at[n], load_sem.at[3 + n])
        copy.start()
        staged.append(copy)
    loads = []
    for n, (src, dst) in enumerate(((l1_in, l1_v), (l2_in, l2_v), (u_in, u_v))):
        copy = pltpu.make_async_copy(src, dst, load_sem.at[n])
        copy.start()
        loads.append(copy)

    barrier = pltpu.get_barrier_semaphore()

    def greet(to):
        pl.semaphore_signal(barrier, inc=1, device_id=to, device_id_type=MESH)

    @pl.when(slab != z)
    def _():
        for sx in range(2):
            for sy in range(2):
                greet(dev(sx, sy, slab, k))

    for dz in range(1, Z):
        greet(dev(x, y, (z + dz) % Z, k))
    for d in range(1, 8):
        greet(dev((x + d % 2) % 2, (y + d // 2 % 2) % 2, z, (k + d // 4) % 2))
    pl.semaphore_wait(barrier, 7 + 2 * (Z - 1))

    own = x * C + c

    def in_columns(b, slot):
        return at(mcol.at[b], slot, span), m_sem.at[b, slot]

    def panel_out(b):
        px, py = z % 2, z // 2
        dst, sem = in_columns(b, own)
        for dz in (2, 3, 1):
            send(panels.at[b], dst, sem, dev(px, py, (z + dz) % Z, k))
        send_or_copy(panels.at[b], dst, sem, dev(px, py, z, k), (x == px) & (y == py))

    def left_out(b):
        dst, sem = at(mrow.at[b], c, span), g_sem.at[b, c]
        for dx, dy in others:
            send(panels.at[b], dst, sem, dev((x + dx) % 2, (y + dy) % 2, z, x))
        send_or_copy(panels.at[b], dst, sem, dev(x, y, z, 1 - k), k == x)

    def columns_in(b):
        for sx in range(2):
            for sy in range(2):
                piece, sem = in_columns(b, sx * C + 2 * sy + k)
                arrived(piece, sem)
                send(piece, piece, sem, dev(x, y, z, 1 - k))

    def columns_arrived(b):
        for sx in range(2):
            for sy in range(2):
                arrived(*in_columns(b, sx * C + 2 * sy + 1 - k))

    def left_arrived(b):
        for n in range(C):
            arrived(at(mrow.at[b], n, span), g_sem.at[b, n])

    def tile_product(b, listing):
        live = live_column(listing, slab * K, K)
        for dy in (1, 0):
            ty = (y + dy) % 2
            columns = pl.ds(pl.multiple_of(ty * 2 * wc, 2 * wc), 2 * wc)
            product = split_dot(x_pair, halves(live * mcol[b, :, columns]), PLAIN)
            for n in range(2):
                abuf[b, 2 * ty + n] = product[:, n * wc:(n + 1) * wc]
            for n, (dx, my) in enumerate(others):
                if my == dy:
                    tx = (x + dx) % 2
                    send(abuf.at[b, 2 * ty + tx], arecv.at[b, n], a_sem.at[b, n], dev(tx, ty, z, k))

    def total(b, mask):
        result = abuf[b, slab]
        for n in range(len(others)):
            arrived(arecv.at[b, n], a_sem.at[b, n])
            result = result + arecv[b, n]
        result = mask * result
        asum[b] = result
        return halves(result)

    def rows_out(b):
        for dy in range(2):
            for dk in range(2):
                ty, tk = (y + dy) % 2, (k + dk) % 2
                src, dst, sem = at(asum.at[b], 2 * ty + tk, span), frow.at[b, slab], f_sem.at[b, slab]
                if dy or dk:
                    send(src, dst, sem, dev(k, ty, z, tk))
                else:
                    send_or_copy(src, dst, sem, dev(k, ty, z, tk), k == x)

    def core_out(b):
        send(at(qbuf.at[b], 1 - k, part), krecv.at[b], k_sem.at[b], dev(x, y, z, 1 - k))

    def core_in(b):
        arrived(krecv.at[b], k_sem.at[b])
        ksum[b] = qbuf[b, pl.ds(pl.multiple_of(k * part, 8), part)] + krecv[b]
        for dz in range(1, Z):
            to = (z + dz) % Z
            send(at(ksum.at[b], to, ch), zrecv.at[b, dz], q_sem.at[b, dz], dev(x, y, to, k))

    def region(b, column, core):
        return qfull.at[column, pl.ds(pl.multiple_of(b * W + core * part, 8), part)]

    def chunk(b, column, core, dz):
        plane = (z + Z - dz) % Z
        return qfull.at[column, pl.ds(pl.multiple_of(b * W + core * part + plane * ch, 8), ch)]

    beside, along, across = 2 * y + 1 - x, 2 * (1 - y) + x, 2 * (1 - y) + 1 - x

    def to_core(piece, sem):
        send(piece, piece, sem, dev(x, y, z, 1 - k))

    def to_near(b, dz):
        piece = chunk(b, slab, k, dz)
        send(piece, piece, gx_sem.at[b, dz], dev(1 - x, y, z, k))
        send(piece, piece, gy_sem.at[b, dz], dev(x, 1 - y, z, k))

    def planes_in(b):
        result = ksum[b, pl.ds(pl.multiple_of(z * ch, 8), ch)]
        for dz in range(1, Z):
            arrived(zrecv.at[b, dz], q_sem.at[b, dz])
            result = result + zrecv[b, dz]
        piece = chunk(b, slab, k, 0)
        piece[...] = result
        for dz in range(1, Z):
            send(piece, piece, gz_sem.at[b, dz], dev(x, y, (z + dz) % Z, k))
        to_near(b, 0)

    def planes_on(b):
        for dz in range(1, Z):
            arrived(chunk(b, slab, k, dz), gz_sem.at[b, dz])
            to_near(b, dz)
        to_core(region(b, slab, k), gc_sem.at[b, 0])

    def near_on(b, dz):
        piece = chunk(b, beside, k, dz)
        arrived(piece, gx_sem.at[b, dz])
        if dz % 2 == 0:
            send(piece, piece, gd_sem.at[b, dz], dev(x, 1 - y, z, k))
        piece = chunk(b, along, k, dz)
        arrived(piece, gy_sem.at[b, dz])
        if dz % 2 == 1:
            send(piece, piece, gd_sem.at[b, dz], dev(1 - x, y, z, k))

    def near_rest(b):
        for dz in range(1, Z):
            near_on(b, dz)
        to_core(region(b, beside, k), gc_sem.at[b, 1])
        to_core(region(b, along, k), gc_sem.at[b, 2])

    def gather_far(b):
        for dz in range(Z):
            arrived(chunk(b, across, k, dz), gd_sem.at[b, dz])
        to_core(region(b, across, k), gc_sem.at[b, 3])

    def gathered(b):
        for n, column in enumerate((slab, beside, along, across)):
            arrived(region(b, column, 1 - k), gc_sem.at[b, n])

    def square(n, src, dst):
        loads[n].wait()
        pair = halves(src[...])
        dst[...] = split_dot(pair, pair, FIRST)

    staged[0].wait()
    panel_out(0)
    send(x_in, x_v, x_sem, dev(1 - x, y, z, 1 - k), k != x)
    staged[1].wait()
    panel_out(1)
    left_out(0)
    square(0, l1_v, d1_out)
    square(1, l2_v, d2_out)
    block_row = 2 * z + k
    row_one, row_two = live_column(list1, block_row * rows, rows), live_column(list2, block_row * rows, rows)
    arrived(x_v, x_sem)
    x_pair = halves(x_v[...])
    columns_in(0)
    columns_arrived(0)
    tile_product(0, list1)
    left_out(1)
    left_arrived(0)
    left_one = halves(row_one * mrow[0])
    loads[2].wait()
    u_pair = halves(u_v[...])
    columns_in(1)
    right_one = total(0, row_one)
    qbuf[0] = split_dot(left_one, right_one, FIRST)
    core_out(0)
    rows_out(0)
    core_in(0)
    columns_arrived(1)
    tile_product(1, list2)
    left_arrived(1)
    left_two = halves(row_two * mrow[1])
    cross = split_dot(right_one, left_two, FIRST)
    for n in range(C):
        qbuf[1, n * wc:(n + 1) * wc] = cross[:, n * wc:(n + 1) * wc]
    core_out(1)
    planes_in(0)
    core_in(1)
    right_two = total(1, row_two)
    qbuf[2] = split_dot(left_two, right_two, FIRST)
    core_out(2)
    rows_out(1)
    planes_in(1)
    planes_on(0)
    core_in(2)
    near_on(0, 0)
    planes_on(1)
    near_rest(0)
    planes_in(2)
    near_on(1, 0)
    near_rest(1)
    gather_far(0)
    for b in range(2):
        for n in range(C):
            arrived(frow.at[b, n], f_sem.at[b, n])
    for n in range(C):
        f_out[:, n * wc:(n + 1) * wc] = -frow[0, n]
        s_out[:, n * wc:(n + 1) * wc] = frow[1, n]
    f_u = split_dot(halves(f_out[...]), u_pair, PLAIN)
    s_out[...] = -live_column(list2, p * rows + c * span, span) * (f_u + s_out[...])
    planes_on(2)
    near_on(2, 0)
    gathered(0)
    for n in range(C):
        d1_out[:, n * wc:(n + 1) * wc] += qfull[n, 0:W]
    d1_u = split_dot(halves(d1_out[...]), u_pair, PLAIN)
    gather_far(1)
    near_rest(2)
    gathered(1)
    for n in range(C):
        for m in range(C):
            wt[n * wc:(n + 1) * wc, m * wc:(m + 1) * wc] = qfull[n, W + m * wc:W + (m + 1) * wc]
    c_out[...] = wt[...] - d1_u
    d2_out[...] -= split_dot(u_pair, halves(c_out[...]), FIRST) + split_dot(
        halves(wt[...]), u_pair, FIRST
    )
    gather_far(2)
    gathered(2)
    for n in range(C):
        d2_out[:, n * wc:(n + 1) * wc] += qfull[n, 2 * W:3 * W]

    assert len(pending) <= nsend
    for copy, when in pending:
        if when is None:
            copy.wait_send()
        else:
            pl.when(when)(copy.wait_send)


def solution(mesh):
    R, C = mesh.shape["prow"], mesh.shape["pcol"]
    g = R // C
    f32, dma = jnp.float32, pltpu.SemaphoreType.DMA

    def general(span, rows, K, W):
        wc, half = W // C, C // 2
        panel = 2 * (C - 1) + (2 * C - 1) * g + 2 * (half - 1) * (g - 1) + half + (half - 1)
        reduced = half + (half - 1) + (C - 1)
        gram = (g - 1) + 2 * (C - 1) + (g - 1) + g * half + g * (half - 1)
        nsend = 2 * panel + 2 * reduced + 3 * gram
        return functools.partial(body, R, C, nsend), [
            pltpu.VMEM((rows, K), f32),
            pltpu.VMEM((W, W), f32),
            pltpu.VMEM((W, W), f32),
            pltpu.VMEM((W, W), f32),
            pltpu.VMEM((2, C, span, W), f32),
            pltpu.VMEM((2, K, W), f32),
            pltpu.VMEM((2, rows, W), f32),
            pltpu.VMEM((2, C, rows, wc), f32),
            pltpu.VMEM((2, half, rows, wc), f32),
            pltpu.VMEM((2, half, rows, wc), f32),
            pltpu.VMEM((2, rows, wc), f32),
            pltpu.VMEM((2, C, span, wc), f32),
            pltpu.VMEM((3, W, wc), f32),
            pltpu.VMEM((3, g, W // g, wc), f32),
            pltpu.VMEM((3, W // g, wc), f32),
            pltpu.VMEM((3, C, W // R, wc), f32),
            pltpu.VMEM((C, 3 * W, wc), f32),
            pltpu.VMEM((W, W), f32),
            dma((4,)),
            dma((nsend,)),
            dma((2, C)),
            dma((2, g * C)),
            dma((2, C)),
            dma((2, half)),
            dma((2, half)),
            dma((2, C)),
            dma((3, g)),
            dma((3, C)),
            dma((3, C)),
            dma((3, g, half)),
            dma((3, g, half)),
            dma((3, g, half)),
        ]

    def paired(span, rows, K, W):
        wc, Z = W // C, R // 2
        nsend = 2 * (4 + 4 + 4 + 3 + 4) + 1 + 3 * (1 + 2 * (Z - 1) + 3 * Z + 4)
        return functools.partial(fast_body, R, C, nsend), [
            pltpu.VMEM((rows, K), f32),
            pltpu.VMEM((W, W), f32),
            pltpu.VMEM((W, W), f32),
            pltpu.VMEM((W, W), f32),
            pltpu.VMEM((2, span, W), f32),
            pltpu.VMEM((2, K, W), f32),
            pltpu.VMEM((2, rows, W), f32),
            pltpu.VMEM((2, C, rows, wc), f32),
            pltpu.VMEM((2, 3, rows, wc), f32),
            pltpu.VMEM((2, rows, wc), f32),
            pltpu.VMEM((2, C, span, wc), f32),
            pltpu.VMEM((3, W, wc), f32),
            pltpu.VMEM((3, W // 2, wc), f32),
            pltpu.VMEM((3, W // 2, wc), f32),
            pltpu.VMEM((3, Z, W // R, wc), f32),
            pltpu.VMEM((C, 3 * W, wc), f32),
            pltpu.VMEM((W, W), f32),
            dma((5,)),
            dma((nsend,)),
            dma(()),
            dma((2, 2 * C)),
            dma((2, C)),
            dma((2, 3)),
            dma((2, C)),
            dma((3,)),
            dma((3, Z)),
            dma((3, Z)),
            dma((3, Z)),
            dma((3, Z)),
            dma((3, Z)),
            dma((3, 4)),
        ]

    def local(inverse_pool, panel_one, panel_two, upper_two, lower_one, lower_two, list_one, list_two):
        span, W = panel_one.shape
        rows, K = inverse_pool.shape
        kernel, scratch = (paired if (g, C) == (2, 4) else general)(span, rows, K, W)
        shapes = ((span, W), (W, W), (span, W), (W, W), (W, W))
        results = pl.pallas_call(
            kernel,
            out_shape=tuple(pltpu.VMEM(shape, f32) for shape in shapes),
            in_specs=[pl.BlockSpec(memory_space=pl.ANY)] * 6
            + [pl.BlockSpec(memory_space=pltpu.SMEM)] * 2,
            out_specs=(pl.BlockSpec(memory_space=pltpu.VMEM),) * 5,
            scratch_shapes=scratch,
            compiler_params=pltpu.CompilerParams(collective_id=0, has_side_effects=True),
        )(inverse_pool, panel_one, panel_two, upper_two, lower_one, lower_two, list_one, list_two)
        return pl.pallas_call(
            write_out,
            out_shape=tuple(jax.ShapeDtypeStruct(shape, f32) for shape in shapes),
            in_specs=[pl.BlockSpec(memory_space=pl.ANY)] * 5,
            out_specs=(pl.BlockSpec(memory_space=pl.ANY),) * 5,
            scratch_shapes=[dma((5,))],
            compiler_params=pltpu.CompilerParams(vmem_limit_bytes=8 * W * W * 4),
        )(*results)

    return jax.shard_map(
        local,
        mesh=mesh,
        in_specs=(
            P("prow", "pcol"),
            P(("prow", "pcol"), None),
            P(("prow", "pcol"), None),
            P(),
            P(),
            P(),
            P(),
            P(),
        ),
        out_specs=(P(("prow", "pcol"), None), P(), P(("prow", "pcol"), None), P(), P()),
        check_vma=False,
    )
```

```python
import functools

import jax
import jax.numpy as jnp
from jax import lax
from jax.experimental import pallas as pl
from jax.experimental.pallas import tpu as pltpu
from jax.sharding import PartitionSpec as P

BLK = 128
MESH = pl.DeviceIdType.MESH


def halves(value):
    high = value.astype(jnp.bfloat16)
    low = (value - high.astype(jnp.float32)).astype(jnp.bfloat16)
    return high, low


def split_dot(left, right, dims):
    def one(a, b):
        return lax.dot_general(a, b, (dims, ((), ())), preferred_element_type=jnp.float32)

    return one(left[0], right[0]) + (one(left[0], right[1]) + one(left[1], right[0]))


PLAIN = ((1,), (0,))
FIRST = ((0,), (0,))


def live_column(listing, first_row, count):
    blocks = (first_row + lax.broadcasted_iota(jnp.int32, (count, 1), 0)) // BLK

    def step(k, hits):
        return jnp.maximum(hits, jnp.where(blocks == listing[k], 1.0, 0.0).astype(jnp.float32))

    return lax.fori_loop(0, listing.shape[0], step, jnp.zeros((count, 1), jnp.float32))


def write_out(*refs):
    sems = refs[-1]
    copies = [pltpu.make_async_copy(refs[k], refs[5 + k], sems.at[k]) for k in range(5)]
    for copy in copies:
        copy.start()
    for copy in copies:
        copy.wait()


def body(
    R, C, nsend,
    x_in, one_in, two_in, u_in, l1_in, l2_in, list1, list2,
    f_out, d1_out, s_out, c_out, d2_out,
    x_v, u_v, l1_v, l2_v, zbuf, mcol, mrow, abuf, arecv, brecv, asum, frow, qbuf, xrecv, xsum, zrecv, qfull, wt,
    load_sem, send_sem, z_sem, m_sem, g_sem, a_sem, b_sem, f_sem, x_sem, q_sem, gz_sem, gx_sem, gy_sem, gc_sem,
):
    g, half = R // C, C // 2
    span, W = one_in.shape
    rows, K = x_in.shape
    wc = W // C
    part, ch = W // g, W // R
    p, c = lax.axis_index("prow"), lax.axis_index("pcol")
    z, i = p // g, p % g
    partner = c + 1 - 2 * (c % 2)
    panels = (one_in, two_in)
    pending = []

    def send(src, dst, recv_sem, to, when=None):
        copy = pltpu.make_async_remote_copy(
            src_ref=src, dst_ref=dst, send_sem=send_sem.at[len(pending)],
            recv_sem=recv_sem, device_id=to, device_id_type=MESH,
        )
        pending.append((copy, when))
        if when is None:
            copy.start()
        else:
            pl.when(when)(copy.start)

    def arrived(dst, recv_sem):
        pltpu.make_async_copy(dst, dst, recv_sem).wait()

    def at(base, index, size):
        return base.at[pl.ds(pl.multiple_of(index * size, 8), size)]

    def plane_peer(dz):
        return (((z + dz) % C) * g + i, c)

    def side_peer(di):
        return (z * g + (i + di) % g, c)

    loads = []
    for k, (src, dst) in enumerate(((l1_in, l1_v), (l2_in, l2_v), (x_in, x_v), (u_in, u_v))):
        copy = pltpu.make_async_copy(src, dst, load_sem.at[k])
        copy.start()
        loads.append(copy)

    barrier = pltpu.get_barrier_semaphore()
    peers = 0
    for dp in range(1, R):
        pl.semaphore_signal(barrier, inc=1, device_id=((p + dp) % R, c), device_id_type=MESH)
        peers += 1
    for di in range(g):
        for dc in range(1, C):
            pl.semaphore_signal(
                barrier, inc=1, device_id=(z * g + (i + di) % g, (c + dc) % C), device_id_type=MESH
            )
            peers += 1
    pl.semaphore_wait(barrier, peers)

    def to_columns(k, src, plane, valid=True):
        own = i * C + c
        dst, sem = at(mcol.at[k], own, span), m_sem.at[k, own]
        send(src, dst, sem, (p, plane), (plane != c) & valid)
        pl.when((plane == c) & valid)(pltpu.make_async_copy(src, dst, sem).start)
        for di in range(1, g):
            to = (z * g + (i + di) % g, plane)
            send(src, dst, sem, to, (plane // 2 == c // 2) & valid)

    def along(k, src, plane, way, valid=True):
        inside = (z + 1 < C) if way > 0 else (z > 0)
        send(src, zbuf.at[k, plane], z_sem.at[k, plane], plane_peer(way % C), inside & valid)

    def far(dy, parity):
        return ((c // 2 + dy) % half) * 2 + parity

    def across(k):
        for dy in range(1, half):
            for parity in range(2):
                slot = i * C + far(dy, parity)
                piece = at(mcol.at[k], slot, span)
                arrived(piece, m_sem.at[k, slot])
                for di in range(1, g):
                    send(piece, piece, m_sem.at[k, slot], side_peer(di))

    def columns_arrived(k):
        for dy in range(half):
            for parity in range(2):
                for di in range(1 if dy else 0, g):
                    slot = ((i + di) % g) * C + far(dy, parity)
                    arrived(at(mcol.at[k], slot, span), m_sem.at[k, slot])

    def to_row(k):
        dst, sem = at(mrow.at[k], c, span), g_sem.at[k, c]
        pltpu.make_async_copy(panels[k], dst, sem).start()
        for dc in range(2, C, 2):
            send(panels[k], dst, sem, (p, (c + dc) % C))
        send(panels[k], dst, sem, (p, partner))

    def row_onward(k):
        for dc in range(2, C, 2):
            other = (c + dc) % C
            piece = at(mrow.at[k], other, span)
            arrived(piece, g_sem.at[k, other])
            send(piece, piece, g_sem.at[k, other], (p, partner))

    def row_arrived(k):
        arrived(at(mrow.at[k], c, span), g_sem.at[k, c])
        for dc in range(0, C, 2):
            other = (partner + dc) % C
            arrived(at(mrow.at[k], other, span), g_sem.at[k, other])

    def tile_product(k, listing):
        columns_arrived(k)
        masked = live_column(listing, c * K, K) * mcol[k]
        product = split_dot(x_pair, halves(masked), PLAIN)
        for cc in range(C):
            abuf[k, cc] = product[:, cc * wc:(cc + 1) * wc]
        for j in range(half):
            send(abuf.at[k, (partner + 2 * j) % C], arecv.at[k, j], a_sem.at[k, j], (p, partner))

    def pair_sum(k):
        for j in list(range(1, half)) + [0]:
            other = (c + 2 * j) % C
            arrived(arecv.at[k, j], a_sem.at[k, j])
            abuf[k, other] = abuf[k, other] + arecv[k, j]
            if j:
                send(abuf.at[k, other], brecv.at[k, j], b_sem.at[k, j], (p, other))

    def total(k, mask):
        result = abuf[k, c]
        for j in range(1, half):
            arrived(brecv.at[k, j], b_sem.at[k, j])
            result = result + brecv[k, j]
        result = mask * result
        asum[k] = result
        return halves(result)

    def rows_out(k):
        for dc in range(1, C):
            other = (c + dc) % C
            send(at(asum.at[k], other, span), frow.at[k, c], f_sem.at[k, c], (p, other))
        frow[k, c] = asum[k, pl.ds(pl.multiple_of(c * span, 8), span)]

    def side_out(b):
        for di in range(1, g):
            other = (i + di) % g
            send(at(qbuf.at[b], other, part), xrecv.at[b, di], x_sem.at[b, di], side_peer(di))

    def side_in(b):
        result = qbuf[b, pl.ds(pl.multiple_of(i * part, 8), part)]
        for di in range(1, g):
            arrived(xrecv.at[b, di], x_sem.at[b, di])
            result = result + xrecv[b, di]
        xsum[b] = result
        for dz in range(1, C):
            send(at(xsum.at[b], (z + dz) % C, ch), zrecv.at[b, dz], q_sem.at[b, dz], plane_peer(dz))

    def block(b, column, side, plane):
        first = b * W + side * part + plane * ch
        return qfull.at[column, pl.ds(pl.multiple_of(first, 8), ch)]

    def block_part(b, column, side):
        return qfull.at[column, pl.ds(pl.multiple_of(b * W + side * part, 8), part)]

    def plane_in(b):
        result = xsum[b, pl.ds(pl.multiple_of(z * ch, 8), ch)]
        for dz in range(1, C):
            arrived(zrecv.at[b, dz], q_sem.at[b, dz])
            result = result + zrecv[b, dz]
        piece = block(b, c, i, z)
        piece[...] = result
        for dz in range(1, C):
            send(piece, piece, gz_sem.at[b, dz], plane_peer(dz))

    def gram_part(b, di, dc, base):
        return block_part(b, (base + C - dc) % C, (i + g - di) % g)

    def to_side(b, dc):
        piece = gram_part(b, 0, dc, c)
        for di in range(1, g):
            send(piece, piece, gx_sem.at[b, di, dc // 2], side_peer(di))

    def to_rows(b, di):
        piece = gram_part(b, di, 0, c)
        for dc in range(2, C, 2):
            send(piece, piece, gy_sem.at[b, di, dc // 2], (p, (c + dc) % C))

    def to_partner(b, di, dc):
        piece = gram_part(b, di, dc, c)
        send(piece, piece, gc_sem.at[b, di, dc // 2], (p, partner))

    def side_arrived(b, di, dc):
        arrived(gram_part(b, di, dc, c), gx_sem.at[b, di, dc // 2])

    def rows_arrived(b, di, dc):
        arrived(gram_part(b, di, dc, c), gy_sem.at[b, di, dc // 2])

    def gather_side(b):
        for dz in range(1, C):
            arrived(block(b, c, i, (z + C - dz) % C), gz_sem.at[b, dz])
        to_side(b, 0)
        to_rows(b, 0)
        to_partner(b, 0, 0)

    def gather_row(b):
        if b == 1:
            for dc in range(2, C, 2):
                rows_arrived(b, 0, dc)
                to_side(b, dc)
                to_partner(b, 0, dc)
        else:
            for di in range(1, g):
                side_arrived(b, di, 0)
                to_rows(b, di)
                to_partner(b, di, 0)

    def gather_core(b):
        if b == 1:
            for di in range(1, g):
                for dc in range(0, C, 2):
                    side_arrived(b, di, dc)
                    to_partner(b, di, dc)
        else:
            for di in range(g):
                for dc in range(2, C, 2):
                    rows_arrived(b, di, dc)
                    to_partner(b, di, dc)

    def gathered(b):
        for di in range(g):
            for dc in range(0, C, 2):
                piece = block_part(b, (partner + C - dc) % C, (i + g - di) % g)
                arrived(piece, gc_sem.at[b, di, dc // 2])

    for k in range(2):
        along(k, panels[k], z, 1)
        along(k, panels[k], z, -1)
        to_columns(k, panels[k], z)
    for k in range(2):
        for dz in range(1, C):
            for way in (1, -1):
                valid = (z >= dz) if way > 0 else (z + dz < C)
                plane = (z + C - way * dz) % C
                src, sem = zbuf.at[k, plane], z_sem.at[k, plane]
                pl.when(valid)(functools.partial(arrived, src, sem))
                if dz < C - 1:
                    along(k, src, plane, way, valid)
                to_columns(k, src, plane, valid)
        to_row(k)
        if k == 0:
            across(0)
            for copy in loads[2:]:
                copy.wait()
            x_pair = halves(x_v[...])
            row_one, row_two = live_column(list1, p * rows, rows), live_column(list2, p * rows, rows)
    row_onward(0)
    tile_product(0, list1)
    across(1)
    pair_sum(0)
    row_onward(1)
    row_arrived(0)
    left = halves(row_one * mrow[0])
    right_one = total(0, row_one)
    qbuf[0] = split_dot(left, right_one, FIRST)
    side_out(0)
    for copy in loads[:2]:
        copy.wait()
    for src, dst in ((l1_v, d1_out), (l2_v, d2_out)):
        pair = halves(src[...])
        dst[...] = split_dot(pair, pair, FIRST)
    tile_product(1, list2)
    pair_sum(1)
    row_arrived(1)
    left = halves(row_two * mrow[1])
    cross = split_dot(right_one, left, FIRST)
    for cc in range(C):
        qbuf[1, cc * wc:(cc + 1) * wc] = cross[:, cc * wc:(cc + 1) * wc]
    side_out(1)
    side_in(0)
    right_two = total(1, row_two)
    qbuf[2] = split_dot(left, right_two, FIRST)
    side_out(2)
    plane_in(0)
    side_in(1)
    gather_side(0)
    plane_in(1)
    side_in(2)
    gather_row(0)
    gather_side(1)
    plane_in(2)
    gather_core(0)
    gather_row(1)
    gather_side(2)
    rows_out(0)
    rows_out(1)
    gather_core(1)
    gather_row(2)

    u_pair = halves(u_v[...])
    gathered(0)
    for cc in range(C):
        d1_out[:, cc * wc:(cc + 1) * wc] += qfull[cc, 0:W]
    d1_u = split_dot(halves(d1_out[...]), u_pair, PLAIN)
    gather_core(2)
    for k in range(2):
        for dc in range(1, C):
            other = (c + dc) % C
            arrived(frow.at[k, other], f_sem.at[k, other])
    for cc in range(C):
        f_out[:, cc * wc:(cc + 1) * wc] = -frow[0, cc]
        s_out[:, cc * wc:(cc + 1) * wc] = frow[1, cc]
    f_u = split_dot(halves(f_out[...]), u_pair, PLAIN)
    s_out[...] = -live_column(list2, p * rows + c * span, span) * (f_u + s_out[...])

    gathered(1)
    for cc in range(C):
        for k in range(C):
            wt[cc * wc:(cc + 1) * wc, k * wc:(k + 1) * wc] = qfull[cc, W + k * wc:W + (k + 1) * wc]
    c_out[...] = wt[...] - d1_u
    d2_out[...] -= split_dot(u_pair, halves(c_out[...]), FIRST) + split_dot(
        halves(wt[...]), u_pair, FIRST
    )
    gathered(2)
    for cc in range(C):
        d2_out[:, cc * wc:(cc + 1) * wc] += qfull[cc, 2 * W:3 * W]

    assert len(pending) <= nsend
    for copy, when in pending:
        if when is None:
            copy.wait_send()
        else:
            pl.when(when)(copy.wait_send)


def fast_body(
    R, C, nsend,
    x_in, one_in, two_in, u_in, l1_in, l2_in, list1, list2,
    f_out, d1_out, s_out, c_out, d2_out,
    x_v, u_v, l1_v, l2_v, panels, mcol, mrow, abuf, arecv, asum, frow, qbuf, krecv, ksum, zrecv, qfull, wt,
    load_sem, send_sem, x_sem, m_sem, g_sem, a_sem, f_sem, k_sem, q_sem, gz_sem, gx_sem, gy_sem, gd_sem, gc_sem,
):
    span, W = one_in.shape
    rows, K = x_in.shape
    wc = W // C
    Z = R // 2
    part, ch = W // 2, W // R
    p, c = lax.axis_index("prow"), lax.axis_index("pcol")
    z, x, y, k = p // 2, p % 2, c // 2, c % 2
    slab = 2 * y + x
    others = ((1, 0), (0, 1), (1, 1))
    pending = []

    def dev(x, y, z, k):
        return (z * 2 + x, y * 2 + k)

    def send(src, dst, recv_sem, to, when=None):
        copy = pltpu.make_async_remote_copy(
            src_ref=src, dst_ref=dst, send_sem=send_sem.at[len(pending)],
            recv_sem=recv_sem, device_id=to, device_id_type=MESH,
        )
        pending.append((copy, when))
        if when is None:
            copy.start()
        else:
            pl.when(when)(copy.start)

    def arrived(dst, recv_sem):
        pltpu.make_async_copy(dst, dst, recv_sem).wait()

    def at(base, index, size):
        return base.at[pl.ds(pl.multiple_of(index * size, 8), size)]

    def send_or_copy(src, dst, sem, to, here):
        send(src, dst, sem, to, jnp.logical_not(here))
        pl.when(here)(pltpu.make_async_copy(src, dst, sem).start)

    pl.when(k == x)(pltpu.make_async_copy(x_in, x_v, x_sem).start)
    staged = []
    for n, src in enumerate((one_in, two_in)):
        copy = pltpu.make_async_copy(src, panels.at[n], load_sem.at[3 + n])
        copy.start()
        staged.append(copy)
    loads = []
    for n, (src, dst) in enumerate(((l1_in, l1_v), (l2_in, l2_v), (u_in, u_v))):
        copy = pltpu.make_async_copy(src, dst, load_sem.at[n])
        copy.start()
        loads.append(copy)

    barrier = pltpu.get_barrier_semaphore()

    def greet(to):
        pl.semaphore_signal(barrier, inc=1, device_id=to, device_id_type=MESH)

    @pl.when(slab != z)
    def _():
        for sx in range(2):
            for sy in range(2):
                greet(dev(sx, sy, slab, k))

    for dz in range(1, Z):
        greet(dev(x, y, (z + dz) % Z, k))
    for d in range(1, 8):
        greet(dev((x + d % 2) % 2, (y + d // 2 % 2) % 2, z, (k + d // 4) % 2))
    pl.semaphore_wait(barrier, 7 + 2 * (Z - 1))

    own = x * C + c

    def in_columns(b, slot):
        return at(mcol.at[b], slot, span), m_sem.at[b, slot]

    def panel_out(b):
        px, py = z % 2, z // 2
        dst, sem = in_columns(b, own)
        for dz in (2, 3, 1):
            send(panels.at[b], dst, sem, dev(px, py, (z + dz) % Z, k))
        send_or_copy(panels.at[b], dst, sem, dev(px, py, z, k), (x == px) & (y == py))

    def left_out(b):
        dst, sem = at(mrow.at[b], c, span), g_sem.at[b, c]
        for dx, dy in others:
            send(panels.at[b], dst, sem, dev((x + dx) % 2, (y + dy) % 2, z, x))
        send_or_copy(panels.at[b], dst, sem, dev(x, y, z, 1 - k), k == x)

    def columns_in(b):
        for sx in range(2):
            for sy in range(2):
                piece, sem = in_columns(b, sx * C + 2 * sy + k)
                arrived(piece, sem)
                send(piece, piece, sem, dev(x, y, z, 1 - k))

    def columns_arrived(b):
        for sx in range(2):
            for sy in range(2):
                arrived(*in_columns(b, sx * C + 2 * sy + 1 - k))

    def left_arrived(b):
        for n in range(C):
            arrived(at(mrow.at[b], n, span), g_sem.at[b, n])

    def tile_product(b, listing):
        live = live_column(listing, slab * K, K)
        for dy in (1, 0):
            ty = (y + dy) % 2
            columns = pl.ds(pl.multiple_of(ty * 2 * wc, 2 * wc), 2 * wc)
            product = split_dot(x_pair, halves(live * mcol[b, :, columns]), PLAIN)
            for n in range(2):
                abuf[b, 2 * ty + n] = product[:, n * wc:(n + 1) * wc]
            for n, (dx, my) in enumerate(others):
                if my == dy:
                    tx = (x + dx) % 2
                    send(abuf.at[b, 2 * ty + tx], arecv.at[b, n], a_sem.at[b, n], dev(tx, ty, z, k))

    def total(b, mask):
        result = abuf[b, slab]
        for n in range(len(others)):
            arrived(arecv.at[b, n], a_sem.at[b, n])
            result = result + arecv[b, n]
        result = mask * result
        asum[b] = result
        return halves(result)

    def rows_out(b):
        for dy in range(2):
            for dk in range(2):
                ty, tk = (y + dy) % 2, (k + dk) % 2
                src, dst, sem = at(asum.at[b], 2 * ty + tk, span), frow.at[b, slab], f_sem.at[b, slab]
                if dy or dk:
                    send(src, dst, sem, dev(k, ty, z, tk))
                else:
                    send_or_copy(src, dst, sem, dev(k, ty, z, tk), k == x)

    def core_out(b):
        send(at(qbuf.at[b], 1 - k, part), krecv.at[b], k_sem.at[b], dev(x, y, z, 1 - k))

    def core_in(b):
        arrived(krecv.at[b], k_sem.at[b])
        ksum[b] = qbuf[b, pl.ds(pl.multiple_of(k * part, 8), part)] + krecv[b]
        for dz in range(1, Z):
            to = (z + dz) % Z
            send(at(ksum.at[b], to, ch), zrecv.at[b, dz], q_sem.at[b, dz], dev(x, y, to, k))

    def region(b, column, core):
        return qfull.at[column, pl.ds(pl.multiple_of(b * W + core * part, 8), part)]

    def chunk(b, column, core, dz):
        plane = (z + Z - dz) % Z
        return qfull.at[column, pl.ds(pl.multiple_of(b * W + core * part + plane * ch, 8), ch)]

    beside, along, across = 2 * y + 1 - x, 2 * (1 - y) + x, 2 * (1 - y) + 1 - x

    def to_core(piece, sem):
        send(piece, piece, sem, dev(x, y, z, 1 - k))

    def to_near(b, dz):
        piece = chunk(b, slab, k, dz)
        send(piece, piece, gx_sem.at[b, dz], dev(1 - x, y, z, k))
        send(piece, piece, gy_sem.at[b, dz], dev(x, 1 - y, z, k))

    def planes_in(b):
        result = ksum[b, pl.ds(pl.multiple_of(z * ch, 8), ch)]
        for dz in range(1, Z):
            arrived(zrecv.at[b, dz], q_sem.at[b, dz])
            result = result + zrecv[b, dz]
        piece = chunk(b, slab, k, 0)
        piece[...] = result
        for dz in range(1, Z):
            send(piece, piece, gz_sem.at[b, dz], dev(x, y, (z + dz) % Z, k))
        to_near(b, 0)

    def planes_on(b):
        for dz in range(1, Z):
            arrived(chunk(b, slab, k, dz), gz_sem.at[b, dz])
            to_near(b, dz)
        to_core(region(b, slab, k), gc_sem.at[b, 0])

    def near_on(b, dz):
        piece = chunk(b, beside, k, dz)
        arrived(piece, gx_sem.at[b, dz])
        if dz % 2 == 0:
            send(piece, piece, gd_sem.at[b, dz], dev(x, 1 - y, z, k))
        piece = chunk(b, along, k, dz)
        arrived(piece, gy_sem.at[b, dz])
        if dz % 2 == 1:
            send(piece, piece, gd_sem.at[b, dz], dev(1 - x, y, z, k))

    def near_rest(b):
        for dz in range(1, Z):
            near_on(b, dz)
        to_core(region(b, beside, k), gc_sem.at[b, 1])
        to_core(region(b, along, k), gc_sem.at[b, 2])

    def gather_far(b):
        for dz in range(Z):
            arrived(chunk(b, across, k, dz), gd_sem.at[b, dz])
        to_core(region(b, across, k), gc_sem.at[b, 3])

    def gathered(b):
        for n, column in enumerate((slab, beside, along, across)):
            arrived(region(b, column, 1 - k), gc_sem.at[b, n])

    def square(n, src, dst):
        loads[n].wait()
        pair = halves(src[...])
        dst[...] = split_dot(pair, pair, FIRST)

    staged[0].wait()
    panel_out(0)
    send(x_in, x_v, x_sem, dev(1 - x, y, z, 1 - k), k != x)
    staged[1].wait()
    panel_out(1)
    left_out(0)
    square(0, l1_v, d1_out)
    square(1, l2_v, d2_out)
    block_row = 2 * z + k
    row_one, row_two = live_column(list1, block_row * rows, rows), live_column(list2, block_row * rows, rows)
    arrived(x_v, x_sem)
    x_pair = halves(x_v[...])
    columns_in(0)
    columns_arrived(0)
    tile_product(0, list1)
    left_out(1)
    left_arrived(0)
    left_one = halves(row_one * mrow[0])
    loads[2].wait()
    u_pair = halves(u_v[...])
    columns_in(1)
    right_one = total(0, row_one)
    qbuf[0] = split_dot(left_one, right_one, FIRST)
    core_out(0)
    rows_out(0)
    core_in(0)
    columns_arrived(1)
    tile_product(1, list2)
    left_arrived(1)
    left_two = halves(row_two * mrow[1])
    cross = split_dot(right_one, left_two, FIRST)
    for n in range(C):
        qbuf[1, n * wc:(n + 1) * wc] = cross[:, n * wc:(n + 1) * wc]
    core_out(1)
    planes_in(0)
    core_in(1)
    right_two = total(1, row_two)
    qbuf[2] = split_dot(left_two, right_two, FIRST)
    core_out(2)
    rows_out(1)
    planes_in(1)
    planes_on(0)
    near_on(0, 0)
    core_in(2)
    planes_on(1)
    near_rest(0)
    planes_in(2)
    near_on(1, 0)
    near_rest(1)
    gather_far(0)
    for b in range(2):
        for n in range(C):
            arrived(frow.at[b, n], f_sem.at[b, n])
    for n in range(C):
        f_out[:, n * wc:(n + 1) * wc] = -frow[0, n]
        s_out[:, n * wc:(n + 1) * wc] = frow[1, n]
    f_u = split_dot(halves(f_out[...]), u_pair, PLAIN)
    s_out[...] = -live_column(list2, p * rows + c * span, span) * (f_u + s_out[...])
    planes_on(2)
    near_on(2, 0)
    gathered(0)
    for n in range(C):
        d1_out[:, n * wc:(n + 1) * wc] += qfull[n, 0:W]
    d1_u = split_dot(halves(d1_out[...]), u_pair, PLAIN)
    d2_out[...] += split_dot(u_pair, halves(d1_u), FIRST)
    gather_far(1)
    near_rest(2)
    gathered(1)
    for n in range(C):
        for m in range(C):
            wt[n * wc:(n + 1) * wc, m * wc:(m + 1) * wc] = qfull[n, W + m * wc:W + (m + 1) * wc]
    c_out[...] = wt[...] - d1_u
    cross = split_dot(u_pair, halves(wt[...]), FIRST)
    d2_out[...] -= cross + cross.T
    gather_far(2)
    gathered(2)
    for n in range(C):
        d2_out[:, n * wc:(n + 1) * wc] += qfull[n, 2 * W:3 * W]

    assert len(pending) <= nsend
    for copy, when in pending:
        if when is None:
            copy.wait_send()
        else:
            pl.when(when)(copy.wait_send)


def solution(mesh):
    R, C = mesh.shape["prow"], mesh.shape["pcol"]
    g = R // C
    f32, dma = jnp.float32, pltpu.SemaphoreType.DMA

    def general(span, rows, K, W):
        wc, half = W // C, C // 2
        panel = 2 * (C - 1) + (2 * C - 1) * g + 2 * (half - 1) * (g - 1) + half + (half - 1)
        reduced = half + (half - 1) + (C - 1)
        gram = (g - 1) + 2 * (C - 1) + (g - 1) + g * half + g * (half - 1)
        nsend = 2 * panel + 2 * reduced + 3 * gram
        return functools.partial(body, R, C, nsend), [
            pltpu.VMEM((rows, K), f32),
            pltpu.VMEM((W, W), f32),
            pltpu.VMEM((W, W), f32),
            pltpu.VMEM((W, W), f32),
            pltpu.VMEM((2, C, span, W), f32),
            pltpu.VMEM((2, K, W), f32),
            pltpu.VMEM((2, rows, W), f32),
            pltpu.VMEM((2, C, rows, wc), f32),
            pltpu.VMEM((2, half, rows, wc), f32),
            pltpu.VMEM((2, half, rows, wc), f32),
            pltpu.VMEM((2, rows, wc), f32),
            pltpu.VMEM((2, C, span, wc), f32),
            pltpu.VMEM((3, W, wc), f32),
            pltpu.VMEM((3, g, W // g, wc), f32),
            pltpu.VMEM((3, W // g, wc), f32),
            pltpu.VMEM((3, C, W // R, wc), f32),
            pltpu.VMEM((C, 3 * W, wc), f32),
            pltpu.VMEM((W, W), f32),
            dma((4,)),
            dma((nsend,)),
            dma((2, C)),
            dma((2, g * C)),
            dma((2, C)),
            dma((2, half)),
            dma((2, half)),
            dma((2, C)),
            dma((3, g)),
            dma((3, C)),
            dma((3, C)),
            dma((3, g, half)),
            dma((3, g, half)),
            dma((3, g, half)),
        ]

    def paired(span, rows, K, W):
        wc, Z = W // C, R // 2
        nsend = 2 * (4 + 4 + 4 + 3 + 4) + 1 + 3 * (1 + 2 * (Z - 1) + 3 * Z + 4)
        return functools.partial(fast_body, R, C, nsend), [
            pltpu.VMEM((rows, K), f32),
            pltpu.VMEM((W, W), f32),
            pltpu.VMEM((W, W), f32),
            pltpu.VMEM((W, W), f32),
            pltpu.VMEM((2, span, W), f32),
            pltpu.VMEM((2, K, W), f32),
            pltpu.VMEM((2, rows, W), f32),
            pltpu.VMEM((2, C, rows, wc), f32),
            pltpu.VMEM((2, 3, rows, wc), f32),
            pltpu.VMEM((2, rows, wc), f32),
            pltpu.VMEM((2, C, span, wc), f32),
            pltpu.VMEM((3, W, wc), f32),
            pltpu.VMEM((3, W // 2, wc), f32),
            pltpu.VMEM((3, W // 2, wc), f32),
            pltpu.VMEM((3, Z, W // R, wc), f32),
            pltpu.VMEM((C, 3 * W, wc), f32),
            pltpu.VMEM((W, W), f32),
            dma((5,)),
            dma((nsend,)),
            dma(()),
            dma((2, 2 * C)),
            dma((2, C)),
            dma((2, 3)),
            dma((2, C)),
            dma((3,)),
            dma((3, Z)),
            dma((3, Z)),
            dma((3, Z)),
            dma((3, Z)),
            dma((3, Z)),
            dma((3, 4)),
        ]

    def local(inverse_pool, panel_one, panel_two, upper_two, lower_one, lower_two, list_one, list_two):
        span, W = panel_one.shape
        rows, K = inverse_pool.shape
        kernel, scratch = (paired if (g, C) == (2, 4) else general)(span, rows, K, W)
        shapes = ((span, W), (W, W), (span, W), (W, W), (W, W))
        results = pl.pallas_call(
            kernel,
            out_shape=tuple(pltpu.VMEM(shape, f32) for shape in shapes),
            in_specs=[pl.BlockSpec(memory_space=pl.ANY)] * 6
            + [pl.BlockSpec(memory_space=pltpu.SMEM)] * 2,
            out_specs=(pl.BlockSpec(memory_space=pltpu.VMEM),) * 5,
            scratch_shapes=scratch,
            compiler_params=pltpu.CompilerParams(collective_id=0, has_side_effects=True),
        )(inverse_pool, panel_one, panel_two, upper_two, lower_one, lower_two, list_one, list_two)
        return pl.pallas_call(
            write_out,
            out_shape=tuple(jax.ShapeDtypeStruct(shape, f32) for shape in shapes),
            in_specs=[pl.BlockSpec(memory_space=pl.ANY)] * 5,
            out_specs=(pl.BlockSpec(memory_space=pl.ANY),) * 5,
            scratch_shapes=[dma((5,))],
            compiler_params=pltpu.CompilerParams(vmem_limit_bytes=8 * W * W * 4),
        )(*results)

    return jax.shard_map(
        local,
        mesh=mesh,
        in_specs=(
            P("prow", "pcol"),
            P(("prow", "pcol"), None),
            P(("prow", "pcol"), None),
            P(),
            P(),
            P(),
            P(),
            P(),
        ),
        out_specs=(P(("prow", "pcol"), None), P(), P(("prow", "pcol"), None), P(), P()),
        check_vma=False,
    )
```
